256 devices in a mesh: events: 8 (over x, z_lo), shells: 32 (over y, z_hi, core).
Axes of the slice: x: 4, y: 4, z: 8 (z_hi: 4, z_lo: 2; z = z_hi * 2 + z_lo), core: 2. Of those that a mesh axis runs over, the one named last changes fastest.
Arguments:
- model: bfloat16 [2097152], P('shells'), may hold values from -6 to 6
- sensitivity: bfloat16 [131072, 64, 128], P(('events', 'shells')), may hold values from -0.1875 to 0.1875
- pick_block: int32 [131072], P(('events', 'shells')), may hold values from 0 to 2047, as said below
- cell_block: int32 [131072], P(('events', 'shells')), may hold values from 0 to 511
- blk_count: int32 [256], P(('events', 'shells')), may hold values from 128 to 512, as said below
- observed: float32 [1048576], P(('events', 'shells')), may hold values from -6 to 6
- pick_weight: float32 [1048576], P(('events', 'shells')), may hold values from 0.2 to 15
- station: int32 [1048576], P(('events', 'shells')), may hold values from 0 to 2047
Outputs:
- gradient: float32 [2097152], P('shells')
- correction: float32 [2048], replicated
- weighted: float32 [1048576], P(('events', 'shells'))
The draws below stay inside these ranges and needn't reach their ends.
Inputs may be any that keep to these rules, and one draw needn't show every extreme that they name: `blk_count`: each device uses its first slots; some device uses all 512 in every draw. The owner of a slot is pick_block // 64. Among the used slots of one device, at most 32 have one owner; in every event group some owner gets exactly 32 from every device of the group.
All inputs are finite; a program needn't handle non-finite values.
Results may differ from the reference program's by a relative error of at most 0.0026.
Values may be sent and summed in bfloat16 or wider, within the bound.
No kernel may reach another device: no remote copies, remote signals or barrier semaphores. Data moves between devices by JAX's collectives and lax.ppermute only.
A program may use at most 64 MiB of HBM per device.

```python
import jax
import jax.numpy as jnp
from jax import lax

PICK_BLK = 64
CELL_BLK = 128
STATIONS = 2048
PBLK_DEV = 64
CBLK_DEV = 512
NBLK = 512
DEVS_ALL = 256
GROUP_PBLK = 2048
PICKS = 1048576
CELLS = 2097152
SLOTS = 131072
PICK_CAP = 32
N_EVENTS = 8
N_SHELLS = 32


def station_table(key):
    return jax.random.randint(jax.random.fold_in(key, 7), (PICKS,), 0, STATIONS, dtype=jnp.int32)


def draw_station(key, part):
    return station_table(key)


def draw_observed(key, part):
    stations_of = station_table(key)
    offsets = jax.random.uniform(jax.random.fold_in(key, 8), (STATIONS,), jnp.float32, -2.0, 2.0)
    scatter_part = jnp.clip(jax.random.normal(jax.random.fold_in(key, 9), (PICKS,), jnp.float32), -4.0, 4.0)
    return offsets[stations_of] + 0.5 * scatter_part


def draw_pick_weight(key, part):
    rising = 1.0 + 2.0 * jnp.arange(PICKS, dtype=jnp.float32) / PICKS
    spread_part = jnp.exp(jax.random.uniform(jax.random.fold_in(key, 10), (PICKS,), jnp.float32, jnp.log(0.2), jnp.log(5.0)))
    return spread_part * rising


def draw_blk_count(key, part):
    counts = jax.random.randint(jax.random.fold_in(key, 11), (DEVS_ALL,), NBLK // 4, NBLK + 1, dtype=jnp.int32)
    shuffle = jax.random.permutation(jax.random.fold_in(key, 12), DEVS_ALL)
    return counts.at[shuffle[0]].set(NBLK)


def draw_pick_block(key, part):
    group_owner = jax.random.randint(jax.random.fold_in(key, 21), (N_EVENTS,), 0, N_SHELLS, dtype=jnp.int32)
    device_keys = jax.random.split(jax.random.fold_in(key, 22), DEVS_ALL)

    def one_device(dev_key, device):
        chosen = group_owner[device // N_SHELLS]
        order = jax.random.permutation(dev_key, (N_SHELLS - 1) * PICK_CAP)[:NBLK - PICK_CAP].astype(jnp.int32)
        others = order // PICK_CAP
        others = others + (others >= chosen).astype(jnp.int32)
        owners = jnp.concatenate([jnp.full((PICK_CAP,), chosen, dtype=jnp.int32), others])
        inside = jax.random.randint(jax.random.fold_in(dev_key, 1), (NBLK,), 0, PBLK_DEV, dtype=jnp.int32)
        return owners * PBLK_DEV + inside
    table = jax.vmap(one_device)(device_keys, jnp.arange(DEVS_ALL, dtype=jnp.int32))
    return table.reshape(SLOTS)


def touch_ends(entries, stream_key, smallest, high):
    longest = entries.shape.index(max(entries.shape))
    spots = []
    for shift in (0, 1):
        where = [jax.random.randint(jax.random.fold_in(stream_key, axis), (), 0, length) for axis, length in enumerate(entries.shape)]
        where[longest] = (where[longest] + shift) % entries.shape[longest]
        spots.append(tuple(where))
    return entries.at[spots[0]].set(smallest).at[spots[1]].set(high)


def steps_of(rng, dims, pieces, smallest, largest):
    factor_of, own = 1.0, jax.random.fold_in(rng, 6)
    for axis_at, blocks in pieces:
        steps = jnp.exp(jax.random.uniform(jax.random.fold_in(own, axis_at), (blocks,), jnp.float32, smallest / len(pieces), largest / len(pieces)))
        factor_of = factor_of * jnp.repeat(steps, dims[axis_at] // blocks).reshape([-1 if axis == axis_at else 1 for axis in range(len(dims))])
    return factor_of


def scatter_about(stream_key, dims, width, reach, shards=(), kind=jnp.bfloat16):
    values = width * jax.random.normal(stream_key, dims, jnp.float32)
    if shards:
        values = values * steps_of(stream_key, dims, shards, -0.22, 0.18)
    return jnp.clip(values, -reach, reach).astype(kind)


def setup_inputs(seed: int = 0) -> dict:
    key_of = jax.random.split(jax.random.key(seed), 9)
    return {
        "model": scatter_about(key_of[0], (CELLS,), 1.0, 6.0, ((0, 32),)),
        "sensitivity": scatter_about(key_of[1], (SLOTS, PICK_BLK, CELL_BLK), (CELL_BLK * max(1, NBLK // PBLK_DEV)) ** -0.5, 0.1875, ((0, 256),)),
        "pick_block": draw_pick_block(jax.random.fold_in(key_of[8], 71), 0),
        "cell_block": touch_ends(jax.random.randint(key_of[3], (SLOTS,), 0, CBLK_DEV), jax.random.fold_in(key_of[3], 1), 0, CBLK_DEV - 1).astype(jnp.int32),
        "blk_count": draw_blk_count(jax.random.fold_in(key_of[8], 71), 0),
        "observed": draw_observed(jax.random.fold_in(key_of[8], 71), 0),
        "pick_weight": draw_pick_weight(jax.random.fold_in(key_of[8], 71), 0),
        "station": draw_station(jax.random.fold_in(key_of[8], 71), 0),
    }


def reference(model, sensitivity, pick_block, cell_block, blk_count, observed, pick_weight, station):
    n_devices = N_EVENTS * N_SHELLS
    blocks_all = sensitivity.reshape(n_devices, NBLK, PICK_BLK, CELL_BLK)
    pick_rows = pick_block.reshape(n_devices, NBLK)
    cell_rows = cell_block.reshape(n_devices, NBLK)
    model_shells = model.reshape(N_SHELLS, CBLK_DEV, CELL_BLK)
    device_ids = jnp.arange(n_devices, dtype=jnp.int32)
    shell_ids = device_ids % N_SHELLS
    event_ids = device_ids // N_SHELLS
    living = (jnp.arange(NBLK, dtype=jnp.int32)[None, :] < blk_count[:, None]).astype(jnp.float32)

    def forward(packed):
        blocks, picks_of, cells_of, shell_id, alive = packed
        rows_used = jnp.take(model_shells, shell_id, axis=0)[cells_of].astype(jnp.float32)
        values = jnp.einsum("kpc,kc->kp", blocks.astype(jnp.float32), rows_used) * alive[:, None]
        return jax.ops.segment_sum(values, picks_of, num_segments=GROUP_PBLK)

    partials = lax.map(forward, (blocks_all, pick_rows, cell_rows, shell_ids, living))
    predicted = partials.reshape(N_EVENTS, N_SHELLS, GROUP_PBLK * PICK_BLK).sum(axis=1).reshape(PICKS)
    misfit = observed - predicted
    numer = jax.ops.segment_sum(pick_weight * misfit, station, num_segments=STATIONS)
    denom = jax.ops.segment_sum(pick_weight, station, num_segments=STATIONS)
    correction = numer / (denom + 1.0)
    weighted = pick_weight * (misfit - correction[station])
    weighted_half = weighted.astype(jnp.bfloat16)
    residual_groups = weighted_half.reshape(N_EVENTS, GROUP_PBLK, PICK_BLK)

    def backward(packed):
        blocks, picks_of, cells_of, event_id, alive = packed
        resid_rows = jnp.take(residual_groups, event_id, axis=0)[picks_of].astype(jnp.float32)
        terms = jnp.einsum("kpc,kp->kc", blocks.astype(jnp.float32), resid_rows) * alive[:, None]
        return jax.ops.segment_sum(terms, cells_of, num_segments=CBLK_DEV)

    grads = lax.map(backward, (blocks_all, pick_rows, cell_rows, event_ids, living))
    gradient = grads.reshape(N_EVENTS, N_SHELLS, CBLK_DEV * CELL_BLK).sum(axis=0).reshape(CELLS)
    return gradient, correction, weighted
```

```python
import functools

import jax
import jax.numpy as jnp
from jax import lax
from jax.experimental import pallas as pl
from jax.experimental.pallas import tpu as pltpu
from jax.sharding import PartitionSpec as P

PICK_BLK = 64
CELL_BLK = 128
STATIONS = 2048
LANES = 128
GROUP = 8
CHUNK = 128
F32 = jnp.float32
BF16 = jnp.bfloat16
NT = (((1,), (1,)), ((), ()))
VMEM_BYTES = 40 << 20


def iota(shape, axis):
    return lax.broadcasted_iota(jnp.int32, shape, axis)


def down(row):
    tall = jnp.broadcast_to(row.astype(F32), (LANES, LANES))
    return jnp.transpose(tall).astype(jnp.int32)


def pick(mask):
    return jnp.where(mask, 1.0, 0.0).astype(BF16)


def two_parts(x):
    high = x.astype(BF16)
    return high, (x - high.astype(F32)).astype(BF16)


def three_parts(x):
    high, rest = x.astype(BF16), x
    rest = x - high.astype(F32)
    mid = rest.astype(BF16)
    return high, mid, (rest - mid.astype(F32)).astype(BF16)


def forward_kernel(count, pick_ref, cell_ref, model_ref, blocks_ref, out_ref, values_ref):
    step = pl.program_id(0)
    cells = model_ref.shape[0]
    cell_down = down(cell_ref[pl.ds(step, 1), :])
    pick_down = down(pick_ref[pl.ds(step, 1), :])
    lane = iota((CHUNK, LANES), 1)
    chosen = jnp.concatenate([pick(cell_down == lane + t) for t in range(0, cells, LANES)], axis=1)
    rows = jnp.dot(chosen, model_ref[...], preferred_element_type=F32)
    lane_g, sub_g = iota((GROUP, LANES), 1), iota((GROUP, LANES), 0)
    parts = []
    for j in range(0, CHUNK, GROUP):
        block = blocks_ref[pl.ds(j, GROUP)].reshape(GROUP * PICK_BLK, CELL_BLK)
        wide = lax.dot_general(rows[j : j + GROUP].astype(BF16), block, NT, preferred_element_type=F32)
        part = jnp.zeros((GROUP, LANES), F32)
        for i in range(GROUP // 2):
            own = sub_g == 2 * i + (lane_g >= PICK_BLK).astype(jnp.int32)
            part = jnp.where(own, wide[:, i * LANES : (i + 1) * LANES], part)
        parts.append(part)
    values = jnp.concatenate(parts, axis=0)
    values = values + pltpu.roll(values, PICK_BLK, 1)
    half = (lane >= PICK_BLK).astype(jnp.int32)
    values = jnp.where((pick_down & 1) == half, values, 0.0)
    high, low = two_parts(values)
    at = pl.ds(pl.multiple_of(step * CHUNK, CHUNK), CHUNK)
    values_ref[at, 0:LANES] = high
    values_ref[at, LANES : 2 * LANES] = low

    @pl.when(step == pl.num_programs(0) - 1)
    def _():
        slots = values_ref.shape[0]
        picks = pick_ref[...]
        used = iota(picks.shape, 0) * LANES + iota(picks.shape, 1) < count[0]
        target = jnp.where(used, picks >> 1, -1)
        both = values_ref[...]
        tile = 2 * LANES
        for t in range(0, out_ref.shape[0], tile):
            hot = jnp.concatenate(
                [pick(iota((tile, LANES), 0) + t == target[r : r + 1]) for r in range(slots // LANES)],
                axis=1,
            )
            sums = jnp.dot(hot, both, preferred_element_type=F32)
            out_ref[t : t + tile, :] = sums[:, :LANES] + sums[:, LANES:]


def stations_kernel(terms_ref, observed_ref, weight_ref, station_ref, misfit_ref, out_ref):
    senders, rows = terms_ref.shape[0], terms_ref.shape[1]
    predicted = terms_ref[0]
    for s in range(1, senders):
        predicted = predicted + terms_ref[s]
    misfit = observed_ref[...] - predicted
    misfit_ref[...] = misfit
    weight = weight_ref[...]
    stations = station_ref[...]
    high, low = stations >> 7, stations & (LANES - 1)
    hi_count = STATIONS // LANES
    pieces = [p.astype(F32) for p in three_parts(weight * misfit) + three_parts(weight)]
    total = jnp.zeros((len(pieces) * hi_count, LANES), F32)
    for r0 in range(0, rows, 8):
        left, right = [], []
        for r in range(r0, r0 + 8):
            own = iota((hi_count, LANES), 0) == high[r : r + 1]
            left.append(
                jnp.concatenate([jnp.where(own, p[r : r + 1], 0.0) for p in pieces], axis=0).astype(BF16)
            )
            right.append(pick(iota((LANES, LANES), 0) == low[r : r + 1]))
        total = total + lax.dot_general(
            jnp.concatenate(left, axis=1), jnp.concatenate(right, axis=1), NT, preferred_element_type=F32
        )
    h = hi_count
    numer = total[0:h] + total[h : 2 * h] + total[2 * h : 3 * h]
    denom = total[3 * h : 4 * h] + total[4 * h : 5 * h] + total[5 * h : 6 * h]
    sums = jnp.concatenate([numer, denom], axis=0)
    for s in range(out_ref.shape[0]):
        out_ref[s] = sums


def spread_kernel(terms_ref, out_ref):
    total = terms_ref[0]
    for s in range(1, terms_ref.shape[0]):
        total = total + terms_ref[s]
    for s in range(out_ref.shape[0]):
        out_ref[s] = total


def weighted_kernel(terms_ref, misfit_ref, weight_ref, station_ref, corr_ref, weighted_ref, out_ref):
    total = terms_ref[0]
    for s in range(1, terms_ref.shape[0]):
        total = total + terms_ref[s]
    hi_count = STATIONS // LANES
    corr = total[:hi_count] / (total[hi_count:] + 1.0)
    corr_ref[...] = corr
    stations = station_ref[...]
    high, low = stations >> 7, stations & (LANES - 1)
    table = jnp.concatenate(three_parts(corr), axis=0)
    found = []
    for r in range(stations.shape[0]):
        hot = pick(iota((LANES, LANES), 0) == low[r : r + 1])
        wide = jnp.dot(table, hot, preferred_element_type=F32)
        wide = (wide[:hi_count] + wide[hi_count : 2 * hi_count]) + wide[2 * hi_count :]
        own = iota((hi_count, LANES), 0) == high[r : r + 1]
        found.append(jnp.sum(jnp.where(own, wide, 0.0), axis=0, keepdims=True))
    weighted = weight_ref[...] * (misfit_ref[...] - jnp.concatenate(found, axis=0))
    weighted_ref[...] = weighted
    half = weighted.astype(BF16)
    for s in range(out_ref.shape[0]):
        out_ref[s] = half


def backward_kernel(count, pick_ref, cell_ref, resid_ref, blocks_ref, out_ref, terms_ref):
    step = pl.program_id(0)
    pick_down = down(pick_ref[pl.ds(step, 1), :])
    lane, sub = iota((CHUNK, LANES), 1), iota((CHUNK, LANES), 0)
    used = step * CHUNK + sub < count[0]
    row_of = jnp.where(used, pick_down >> 1, -1)
    chosen = jnp.concatenate(
        [pick(row_of == lane + t) for t in range(0, resid_ref.shape[0], LANES)], axis=1
    )
    resid = jnp.dot(chosen, resid_ref[...], preferred_element_type=F32)
    parity = sub & 1
    half = (lane >= PICK_BLK).astype(jnp.int32)
    resid = jnp.where((pick_down & 1) == parity, resid, pltpu.roll(resid, PICK_BLK, 1))
    resid = jnp.where(half == parity, resid, 0.0)
    sub_g = iota((GROUP, LANES), 0)
    parts = []
    for j in range(0, CHUNK, GROUP):
        block = blocks_ref[pl.ds(j, GROUP)].reshape(GROUP * PICK_BLK, CELL_BLK)
        mine = resid[j : j + GROUP]
        wide = jnp.concatenate(
            [jnp.where(sub_g >> 1 == i, mine, 0.0) for i in range(GROUP // 2)], axis=1
        ).astype(BF16)
        parts.append(jnp.dot(wide, block, preferred_element_type=F32))
    high, low = two_parts(jnp.concatenate(parts, axis=0))
    at = pl.ds(pl.multiple_of(step * CHUNK, CHUNK), CHUNK)
    terms_ref[at, 0:LANES] = high
    terms_ref[at, LANES : 2 * LANES] = low

    @pl.when(step == pl.num_programs(0) - 1)
    def _():
        slots = terms_ref.shape[0]
        cells_of = cell_ref[...]
        both = terms_ref[...]
        tile = 2 * LANES
        for t in range(0, out_ref.shape[1], tile):
            hot = jnp.concatenate(
                [pick(iota((tile, LANES), 0) + t == cells_of[r : r + 1]) for r in range(slots // LANES)],
                axis=1,
            )
            sums = jnp.dot(hot, both, preferred_element_type=F32)
            sums = (sums[:, :LANES] + sums[:, LANES:]).astype(BF16)
            for s in range(out_ref.shape[0]):
                out_ref[s, t : t + tile, :] = sums


def gradient_kernel(terms_ref, out_ref):
    total = terms_ref[0].astype(F32)
    for s in range(1, terms_ref.shape[0]):
        total = total + terms_ref[s].astype(F32)
    out_ref[...] = total


def whole(shape):
    return pl.BlockSpec(shape, lambda *_: (0,) * len(shape))


def simple(kernel, out_shape, name):
    return pl.pallas_call(
        kernel,
        out_shape=out_shape,
        compiler_params=pltpu.CompilerParams(vmem_limit_bytes=VMEM_BYTES),
        name=name,
    )


def swap(x, axis):
    return lax.all_to_all(x, axis, 0, 0, tiled=True)


def slot_call(kernel, tables, blocks, out_shape, count, name):
    slots = blocks.shape[0]
    return pl.pallas_call(
        kernel,
        grid_spec=pltpu.PrefetchScalarGridSpec(
            num_scalar_prefetch=1,
            grid=(slots // CHUNK,),
            in_specs=[whole(t.shape) for t in tables]
            + [pl.BlockSpec((CHUNK, PICK_BLK, CELL_BLK), lambda i, c: (i, 0, 0))],
            out_specs=whole(out_shape.shape),
            scratch_shapes=[pltpu.VMEM((slots, 2 * LANES), BF16)],
        ),
        out_shape=out_shape,
        compiler_params=pltpu.CompilerParams(
            dimension_semantics=("arbitrary",), vmem_limit_bytes=VMEM_BYTES
        ),
        name=name,
    )(count, *tables, blocks)


def local(model, sensitivity, pick_block, cell_block, blk_count, observed, pick_weight, station):
    shells, events = lax.axis_size("shells"), lax.axis_size("events")
    picks_of = pick_block.reshape(-1, LANES)
    cells_of = cell_block.reshape(-1, LANES)
    model_rows = model.reshape(-1, CELL_BLK)
    observed, weight = observed.reshape(-1, LANES), pick_weight.reshape(-1, LANES)
    station = station.reshape(-1, LANES)
    own_rows = observed.shape[0]
    group_rows = own_rows * shells
    stat_rows = 2 * STATIONS // LANES
    shape = jax.ShapeDtypeStruct

    partials = slot_call(
        forward_kernel,
        (picks_of, cells_of, model_rows),
        sensitivity,
        shape((group_rows, LANES), F32),
        blk_count,
        "forward",
    )
    partials = swap(partials.reshape(shells, own_rows, LANES), "shells")
    misfit, stats = simple(
        stations_kernel,
        (shape((own_rows, LANES), F32), shape((shells, stat_rows, LANES), F32)),
        "stations",
    )(partials, observed, weight, station)
    stats = swap(stats, "shells")
    stats = simple(spread_kernel, shape((events, stat_rows, LANES), F32), "spread")(stats)
    stats = swap(stats, "events")
    correction, weighted, halves = simple(
        weighted_kernel,
        (
            shape((STATIONS // LANES, LANES), F32),
            shape((own_rows, LANES), F32),
            shape((shells, own_rows, LANES), BF16),
        ),
        "weighted",
    )(stats, misfit, weight, station)
    halves = swap(halves, "shells").reshape(group_rows, LANES)
    grads = slot_call(
        backward_kernel,
        (picks_of, cells_of, halves),
        sensitivity,
        shape((events,) + model_rows.shape, BF16),
        blk_count,
        "backward",
    )
    grads = swap(grads, "events")
    gradient = simple(gradient_kernel, shape(model_rows.shape, F32), "gradient")(grads)
    return (gradient.reshape(-1), correction.reshape(-1), weighted.reshape(-1))


def solution(mesh):
    both = P(("events", "shells"))
    placed = (P("shells"), P(("events", "shells"), None, None)) + (both,) * 6
    return jax.shard_map(
        local,
        mesh=mesh,
        in_specs=placed,
        out_specs=(P("shells"), P(), both),
        check_vma=False,
    )
```

```python
import itertools

import jax
import jax.numpy as jnp
from jax import lax
from jax.experimental import pallas as pl
from jax.experimental.pallas import tpu as pltpu
from jax.sharding import PartitionSpec as P

PICK_BLK = 64
CELL_BLK = 128
STATIONS = 2048
LANES = 128
GROUP = 8
CHUNK = 128
F32 = jnp.float32
BF16 = jnp.bfloat16
NT = (((1,), (1,)), ((), ()))
VMEM_BYTES = 40 << 20


def iota(shape, axis):
    return lax.broadcasted_iota(jnp.int32, shape, axis)


def down(row):
    tall = jnp.broadcast_to(row.astype(F32), (LANES, LANES))
    return jnp.transpose(tall).astype(jnp.int32)


def pick(mask):
    return jnp.where(mask, 1.0, 0.0).astype(BF16)


def two_parts(x):
    high = x.astype(BF16)
    return high, (x - high.astype(F32)).astype(BF16)


def three_parts(x):
    high, rest = x.astype(BF16), x
    rest = x - high.astype(F32)
    mid = rest.astype(BF16)
    return high, mid, (rest - mid.astype(F32)).astype(BF16)


def forward_kernel(count_hbm, pick_hbm, cell_hbm, model_hbm, blocks_hbm, out_ref, blocks_ref, used_ref,
                   count, pick_ref, cell_ref, model_ref, values_ref, table_sems, block_sems):
    slots, cells = blocks_ref.shape[0], model_ref.shape[0]
    tables = [
        pltpu.make_async_copy(src, dst, table_sems.at[n])
        for n, (src, dst) in enumerate(
            [(cell_hbm, cell_ref), (model_hbm, model_ref), (pick_hbm, pick_ref), (count_hbm, count)]
        )
    ]
    for copy in tables:
        copy.start()
    copies = []
    for n in range(slots // CHUNK):
        at = pl.ds(n * CHUNK, CHUNK)
        copies.append(pltpu.make_async_copy(blocks_hbm.at[at], blocks_ref.at[at], block_sems.at[n]))
        copies[-1].start()
    for copy in tables:
        copy.wait()
    lane = iota((CHUNK, LANES), 1)
    lane_g, sub_g = iota((GROUP, LANES), 1), iota((GROUP, LANES), 0)
    half = (lane >= PICK_BLK).astype(jnp.int32)
    rows = []
    for n in range(slots // CHUNK):
        cell_down = down(cell_ref[n : n + 1, :])
        chosen = jnp.concatenate([pick(cell_down == lane + t) for t in range(0, cells, LANES)], axis=1)
        rows.append(jnp.dot(chosen, model_ref[...], preferred_element_type=F32))
    for n in range(slots // CHUNK):
        copies[n].wait()
        pick_down = down(pick_ref[n : n + 1, :])
        parts = []
        for j in range(0, CHUNK, GROUP):
            block = blocks_ref[n * CHUNK + j : n * CHUNK + j + GROUP].reshape(GROUP * PICK_BLK, CELL_BLK)
            wide = lax.dot_general(
                rows[n][j : j + GROUP].astype(BF16), block, NT, preferred_element_type=F32
            )
            part = jnp.zeros((GROUP, LANES), F32)
            for i in range(GROUP // 2):
                own = sub_g == 2 * i + (lane_g >= PICK_BLK).astype(jnp.int32)
                part = jnp.where(own, wide[:, i * LANES : (i + 1) * LANES], part)
            parts.append(part)
        values = jnp.concatenate(parts, axis=0)
        values = values + pltpu.roll(values, PICK_BLK, 1)
        values = jnp.where((pick_down & 1) == half, values, 0.0)
        high, low = two_parts(values)
        values_ref[n * CHUNK : (n + 1) * CHUNK, 0:LANES] = high
        values_ref[n * CHUNK : (n + 1) * CHUNK, LANES : 2 * LANES] = low
    picks = pick_ref[...]
    used = iota(picks.shape, 0) * LANES + iota(picks.shape, 1) < count[0]
    picks = jnp.where(used, picks, -1)
    used_ref[...] = picks
    target = picks >> 1
    both = values_ref[...]
    tile = 2 * LANES
    for t in range(0, out_ref.shape[0], tile):
        hot = jnp.concatenate(
            [pick(iota((tile, LANES), 0) + t == target[r : r + 1]) for r in range(slots // LANES)],
            axis=1,
        )
        sums = jnp.dot(hot, both, preferred_element_type=F32)
        out_ref[t : t + tile, :] = sums[:, :LANES] + sums[:, LANES:]


def stations_kernel(terms_ref, observed_ref, weight_ref, station_ref, misfit_ref, out_ref):
    senders, rows = terms_ref.shape[0], terms_ref.shape[1]
    predicted = terms_ref[0]
    for s in range(1, senders):
        predicted = predicted + terms_ref[s]
    misfit = observed_ref[...] - predicted
    misfit_ref[...] = misfit
    weight = weight_ref[...]
    stations = station_ref[...]
    high, low = stations >> 7, stations & (LANES - 1)
    hi_count = STATIONS // LANES
    pieces = [p.astype(F32) for p in three_parts(weight * misfit) + three_parts(weight)]
    total = jnp.zeros((len(pieces) * hi_count, LANES), F32)
    for r0 in range(0, rows, 8):
        left, right = [], []
        for r in range(r0, r0 + 8):
            own = iota((hi_count, LANES), 0) == high[r : r + 1]
            left.append(
                jnp.concatenate([jnp.where(own, p[r : r + 1], 0.0) for p in pieces], axis=0).astype(BF16)
            )
            right.append(pick(iota((LANES, LANES), 0) == low[r : r + 1]))
        total = total + lax.dot_general(
            jnp.concatenate(left, axis=1), jnp.concatenate(right, axis=1), NT, preferred_element_type=F32
        )
    h = hi_count
    numer = total[0:h] + total[h : 2 * h] + total[2 * h : 3 * h]
    denom = total[3 * h : 4 * h] + total[4 * h : 5 * h] + total[5 * h : 6 * h]
    sums = jnp.concatenate([numer, denom], axis=0)
    for s in range(out_ref.shape[0]):
        out_ref[s] = sums


def spread_kernel(terms_ref, out_ref):
    total = terms_ref[0]
    for s in range(1, terms_ref.shape[0]):
        total = total + terms_ref[s]
    for s in range(out_ref.shape[0]):
        out_ref[s] = total


def weighted_kernel(terms_ref, misfit_ref, weight_ref, station_ref, corr_ref, weighted_ref, out_ref):
    total = terms_ref[0]
    for s in range(1, terms_ref.shape[0]):
        total = total + terms_ref[s]
    hi_count = STATIONS // LANES
    corr = total[:hi_count] / (total[hi_count:] + 1.0)
    corr_ref[...] = corr
    stations = station_ref[...]
    high, low = stations >> 7, stations & (LANES - 1)
    table = jnp.concatenate(three_parts(corr), axis=0)
    found = []
    for r in range(stations.shape[0]):
        hot = pick(iota((LANES, LANES), 0) == low[r : r + 1])
        wide = jnp.dot(table, hot, preferred_element_type=F32)
        wide = (wide[:hi_count] + wide[hi_count : 2 * hi_count]) + wide[2 * hi_count :]
        own = iota((hi_count, LANES), 0) == high[r : r + 1]
        found.append(jnp.sum(jnp.where(own, wide, 0.0), axis=0, keepdims=True))
    weighted = weight_ref[...] * (misfit_ref[...] - jnp.concatenate(found, axis=0))
    weighted_ref[...] = weighted
    half = weighted.astype(BF16)
    for s in range(out_ref.shape[0]):
        out_ref[s] = half


def backward_kernel(pick_ref, cell_ref, resid_ref, blocks_ref, out_ref, terms_ref):
    slots = blocks_ref.shape[0]
    lane, sub = iota((CHUNK, LANES), 1), iota((CHUNK, LANES), 0)
    sub_g = iota((GROUP, LANES), 0)
    parity = sub & 1
    half = (lane >= PICK_BLK).astype(jnp.int32)
    for n in range(slots // CHUNK):
        pick_down = down(pick_ref[n : n + 1, :])
        row_of = pick_down >> 1
        chosen = jnp.concatenate(
            [pick(row_of == lane + t) for t in range(0, resid_ref.shape[0], LANES)], axis=1
        )
        resid = jnp.dot(chosen, resid_ref[...], preferred_element_type=F32)
        resid = jnp.where((pick_down & 1) == parity, resid, pltpu.roll(resid, PICK_BLK, 1))
        resid = jnp.where(half == parity, resid, 0.0)
        parts = []
        for j in range(0, CHUNK, GROUP):
            block = blocks_ref[n * CHUNK + j : n * CHUNK + j + GROUP].reshape(GROUP * PICK_BLK, CELL_BLK)
            mine = resid[j : j + GROUP]
            wide = jnp.concatenate(
                [jnp.where(sub_g >> 1 == i, mine, 0.0) for i in range(GROUP // 2)], axis=1
            ).astype(BF16)
            parts.append(jnp.dot(wide, block, preferred_element_type=F32))
        high, low = two_parts(jnp.concatenate(parts, axis=0))
        terms_ref[n * CHUNK : (n + 1) * CHUNK, 0:LANES] = high
        terms_ref[n * CHUNK : (n + 1) * CHUNK, LANES : 2 * LANES] = low
    cells_of = cell_ref[...]
    both = terms_ref[...]
    tile = 2 * LANES
    for t in range(0, out_ref.shape[1], tile):
        hot = jnp.concatenate(
            [pick(iota((tile, LANES), 0) + t == cells_of[r : r + 1]) for r in range(slots // LANES)],
            axis=1,
        )
        sums = jnp.dot(hot, both, preferred_element_type=F32)
        sums = (sums[:, :LANES] + sums[:, LANES:]).astype(BF16)
        for s in range(out_ref.shape[0]):
            out_ref[s, t : t + tile, :] = sums


def gradient_kernel(terms_ref, out_ref):
    total = terms_ref[0].astype(F32)
    for s in range(1, terms_ref.shape[0]):
        total = total + terms_ref[s].astype(F32)
    out_ref[...] = total


def simple(kernel, out_shape, name, **more):
    return pl.pallas_call(
        kernel,
        out_shape=out_shape,
        compiler_params=pltpu.CompilerParams(vmem_limit_bytes=VMEM_BYTES),
        name=name,
        **more,
    )


def swap(x, axis, groups=None):
    return lax.all_to_all(x, axis, 0, 0, tiled=True, axis_index_groups=groups)


def torus_groups():
    lines, planes = {}, {}
    for x, zl, y, zh, c in itertools.product(range(4), range(2), range(4), range(4), range(2)):
        flat = (x * 2 + zl) * 32 + y * 8 + zh * 2 + c
        lines.setdefault((x, y), []).append(flat)
        planes.setdefault((zl, zh, c), []).append(flat)
    return list(lines.values()), list(planes.values())


def local(model, sensitivity, pick_block, cell_block, blk_count, observed, pick_weight, station):
    shells, events = lax.axis_size("shells"), lax.axis_size("events")
    picks_of = pick_block.reshape(-1, LANES)
    cells_of = cell_block.reshape(-1, LANES)
    model_rows = model.reshape(-1, CELL_BLK)
    observed, weight = observed.reshape(-1, LANES), pick_weight.reshape(-1, LANES)
    station = station.reshape(-1, LANES)
    own_rows = observed.shape[0]
    group_rows = own_rows * shells
    stat_rows = 2 * STATIONS // LANES
    shape = jax.ShapeDtypeStruct

    outside = pl.BlockSpec(memory_space=pltpu.HBM)
    lines, planes = torus_groups()
    devices = ("events", "shells")

    partials, blocks, used_picks = pl.pallas_call(
        forward_kernel,
        in_specs=[outside] * 5,
        out_specs=(pl.BlockSpec(memory_space=pltpu.VMEM),) * 3,
        out_shape=(
            shape((group_rows, LANES), F32),
            shape(sensitivity.shape, BF16),
            shape(picks_of.shape, jnp.int32),
        ),
        scratch_shapes=[
            pltpu.SMEM((1,), jnp.int32),
            pltpu.VMEM(picks_of.shape, jnp.int32),
            pltpu.VMEM(cells_of.shape, jnp.int32),
            pltpu.VMEM(model_rows.shape, BF16),
            pltpu.VMEM((sensitivity.shape[0], 2 * LANES), BF16),
            pltpu.SemaphoreType.DMA((4,)),
            pltpu.SemaphoreType.DMA((sensitivity.shape[0] // CHUNK,)),
        ],
        compiler_params=pltpu.CompilerParams(vmem_limit_bytes=VMEM_BYTES),
        name="forward",
    )(blk_count, picks_of, cells_of, model_rows, sensitivity)
    partials = swap(partials.reshape(shells, own_rows, LANES), "shells")
    misfit, stats = simple(
        stations_kernel,
        (shape((own_rows, LANES), F32), shape((len(lines[0]), stat_rows, LANES), F32)),
        "stations",
    )(partials, observed, weight, station)
    stats = swap(stats, devices, lines)
    stats = simple(spread_kernel, shape((len(planes[0]), stat_rows, LANES), F32), "spread")(stats)
    stats = swap(stats, devices, planes)
    correction, weighted, halves = simple(
        weighted_kernel,
        (
            shape((STATIONS // LANES, LANES), F32),
            shape((own_rows, LANES), F32),
            shape((shells, own_rows, LANES), BF16),
        ),
        "weighted",
    )(stats, misfit, weight, station)
    halves = swap(halves, "shells").reshape(group_rows, LANES)
    grads = simple(
        backward_kernel,
        shape((events,) + model_rows.shape, BF16),
        "backward",
        scratch_shapes=[pltpu.VMEM((sensitivity.shape[0], 2 * LANES), BF16)],
    )(used_picks, cells_of, halves, blocks)
    grads = swap(grads, "events")
    gradient = simple(gradient_kernel, shape(model_rows.shape, F32), "gradient")(grads)
    return (gradient.reshape(-1), correction.reshape(-1), weighted.reshape(-1))


def solution(mesh):
    both = P(("events", "shells"))
    placed = (P("shells"), P(("events", "shells"), None, None)) + (both,) * 6
    return jax.shard_map(
        local,
        mesh=mesh,
        in_specs=placed,
        out_specs=(P("shells"), P(), both),
        check_vma=False,
    )
```

```python
import itertools

import jax
import jax.numpy as jnp
from jax import lax
from jax.experimental import pallas as pl
from jax.experimental.pallas import tpu as pltpu
from jax.sharding import PartitionSpec as P

PICK_BLK = 64
CELL_BLK = 128
STATIONS = 2048
LANES = 128
GROUP = 8
CHUNK = 128
F32 = jnp.float32
BF16 = jnp.bfloat16
NT = (((1,), (1,)), ((), ()))
TN = (((0,), (0,)), ((), ()))
SLOT_CAP = 32
VMEM_BYTES = 40 << 20


def iota(shape, axis):
    return lax.broadcasted_iota(jnp.int32, shape, axis)


def down(row):
    tall = jnp.broadcast_to(row.astype(F32), (LANES, LANES))
    return jnp.transpose(tall).astype(jnp.int32)


def pick(mask):
    return jnp.where(mask, 1.0, 0.0).astype(BF16)


def two_parts(x):
    high = x.astype(BF16)
    return high, (x - high.astype(F32)).astype(BF16)


def three_parts(x):
    high, rest = x.astype(BF16), x
    rest = x - high.astype(F32)
    mid = rest.astype(BF16)
    return high, mid, (rest - mid.astype(F32)).astype(BF16)


def forward_kernel(count_hbm, pick_hbm, cell_hbm, model_hbm, blocks_hbm, out_ref, blocks_ref, code_ref,
                   count, pick_ref, cell_ref, model_ref, values_ref, hot_ref, table_sems, block_sems):
    slots, cells = blocks_ref.shape[0], model_ref.shape[0]
    owners = out_ref.shape[0]
    chunks = range(slots // CHUNK)
    tables = [
        pltpu.make_async_copy(src, dst, table_sems.at[n])
        for n, (src, dst) in enumerate(
            [(count_hbm, count), (pick_hbm, pick_ref), (cell_hbm, cell_ref), (model_hbm, model_ref)]
        )
    ]
    for copy in tables:
        copy.start()
    copies = []
    piece = slots // block_sems.shape[0]
    for n in range(slots // piece):
        at = pl.ds(n * piece, piece)
        copies.append(pltpu.make_async_copy(blocks_hbm.at[at], blocks_ref.at[at], block_sems.at[n]))
        copies[-1].start()
    for copy in tables:
        copy.wait()
    lane, sub = iota((CHUNK, LANES), 1), iota((CHUNK, LANES), 0)
    half = (lane >= PICK_BLK).astype(jnp.int32)

    before, every = pick(sub < lane), jnp.ones((CHUNK, LANES), BF16)
    seen = jnp.zeros((owners, LANES), F32)
    index = jnp.zeros((owners * 8, LANES), F32)
    codes, code_down, rows = [], [], []
    for n in chunks:
        picks = pick_ref[n : n + 1, :]
        used = n * CHUNK + iota((1, LANES), 1) < count[0]
        owner, inside = picks >> 6, picks & (PICK_BLK - 1)
        mine = jnp.logical_and(iota((owners, LANES), 0) == owner, used)
        ones = pick(mine)
        ahead = seen + jnp.dot(ones, before, preferred_element_type=F32)
        seen = seen + jnp.dot(ones, every, preferred_element_type=F32)
        rank = jnp.sum(jnp.where(mine, ahead, 0.0), axis=0, keepdims=True).astype(jnp.int32)
        code = jnp.where(used, owner * SLOT_CAP + rank, -1)
        codes.append(code)
        code_ref[n : n + 1, :] = code
        code_down.append(down(code))
        cell_down = down(cell_ref[n : n + 1, :])
        chosen = jnp.concatenate([pick(cell_down == lane + t) for t in range(0, cells, LANES)], axis=1)
        rows.append(jnp.dot(chosen, model_ref[...], preferred_element_type=F32))
        tagged = jnp.logical_and(iota((owners * 8, LANES), 0) >> 3 == owner, used)
        tagged = jnp.where(tagged, (inside + 1).astype(F32), 0.0).astype(BF16)
        ranked = pick((code_down[n] & (SLOT_CAP - 1)) == lane)
        index = index + jnp.dot(tagged, ranked, preferred_element_type=F32)
        hot_ref[:, n * CHUNK : (n + 1) * CHUNK] = pick(iota((hot_ref.shape[0], LANES), 0) == code >> 1)
    out_ref[:, SLOT_CAP:, :] = index.astype(BF16).reshape(owners, 8, LANES)

    lane_g, sub_g = iota((GROUP, LANES), 1), iota((GROUP, LANES), 0)
    for n in chunks:
        parts = []
        for j in range(0, CHUNK, GROUP):
            first = n * CHUNK + j
            if first % piece == 0:
                copies[first // piece].wait()
            block = blocks_ref[first : first + GROUP].reshape(GROUP * PICK_BLK, CELL_BLK)
            wide = lax.dot_general(
                rows[n][j : j + GROUP].astype(BF16), block, NT, preferred_element_type=F32
            )
            part = jnp.zeros((GROUP, LANES), F32)
            for i in range(GROUP // 2):
                own = sub_g == 2 * i + (lane_g >= PICK_BLK).astype(jnp.int32)
                part = jnp.where(own, wide[:, i * LANES : (i + 1) * LANES], part)
            parts.append(part)
        values = jnp.concatenate(parts, axis=0)
        values = values + pltpu.roll(values, PICK_BLK, 1)
        values = jnp.where((code_down[n] & 1) == half, values, 0.0)
        high, low = two_parts(values)
        values_ref[n * CHUNK : (n + 1) * CHUNK, 0:LANES] = high
        values_ref[n * CHUNK : (n + 1) * CHUNK, LANES : 2 * LANES] = low
    placed = jnp.dot(hot_ref[...], values_ref[...], preferred_element_type=F32).astype(BF16)
    q = SLOT_CAP // 2
    out_ref[:, 0:q, :] = placed[:, :LANES].reshape(owners, q, LANES)
    out_ref[:, q : 2 * q, :] = placed[:, LANES:].reshape(owners, q, LANES)


def stations_kernel(terms_ref, observed_ref, weight_ref, station_ref, misfit_ref, place_ref, out_ref):
    senders, rows = terms_ref.shape[0], observed_ref.shape[0]
    q = SLOT_CAP // 2
    flat = senders * q
    lane, sub = iota((flat, LANES), 1), iota((flat, LANES), 0)
    half = (lane >= PICK_BLK).astype(jnp.int32)
    index = terms_ref[:, SLOT_CAP:, :].astype(F32)
    index = jnp.concatenate([index] * (q // 8), axis=1).reshape(flat, LANES)
    every = jnp.ones((LANES, LANES), BF16)
    total = jnp.zeros((LANES, 2 * LANES), F32)
    pieces = [terms_ref[:, n * q : (n + 1) * q, :].astype(F32).reshape(flat, LANES) for n in (0, 1)]
    rolled = [pltpu.roll(p, PICK_BLK, 1) for p in pieces]
    for h in (0, 1):
        own = jnp.where(lane == 2 * (sub & (q - 1)) + h, index, 0.0).astype(BF16)
        place = jnp.dot(own, every, preferred_element_type=F32).astype(jnp.int32) - 1
        place_ref[h] = place
        hot = pick(place >> 1 == lane)
        terms = [
            jnp.where((place & 1) == half, jnp.where(half == h, p, r), 0.0).astype(BF16)
            for p, r in zip(pieces, rolled)
        ]
        total = total + lax.dot_general(
            hot, jnp.concatenate(terms, axis=1), TN, preferred_element_type=F32
        )
    predicted = total[:rows, :LANES] + total[:rows, LANES:]
    misfit = observed_ref[...] - predicted
    misfit_ref[...] = misfit
    weight = weight_ref[...]
    stations = station_ref[...]
    high, low = stations >> 7, stations & (LANES - 1)
    hi_count = STATIONS // LANES
    pieces = [p.astype(F32) for p in three_parts(weight * misfit) + three_parts(weight)]
    total = jnp.zeros((len(pieces) * hi_count, LANES), F32)
    for r0 in range(0, rows, 8):
        left, right = [], []
        for r in range(r0, r0 + 8):
            own = iota((hi_count, LANES), 0) == high[r : r + 1]
            left.append(
                jnp.concatenate([jnp.where(own, p[r : r + 1], 0.0) for p in pieces], axis=0).astype(BF16)
            )
            right.append(pick(iota((LANES, LANES), 0) == low[r : r + 1]))
        total = total + lax.dot_general(
            jnp.concatenate(left, axis=1), jnp.concatenate(right, axis=1), NT, preferred_element_type=F32
        )
    h = hi_count
    numer = total[0:h] + total[h : 2 * h] + total[2 * h : 3 * h]
    denom = total[3 * h : 4 * h] + total[4 * h : 5 * h] + total[5 * h : 6 * h]
    sums = jnp.concatenate([numer, denom], axis=0)
    for s in range(out_ref.shape[0]):
        out_ref[s] = sums


def spread_kernel(terms_ref, out_ref):
    total = terms_ref[0]
    for s in range(1, terms_ref.shape[0]):
        total = total + terms_ref[s]
    for s in range(out_ref.shape[0]):
        out_ref[s] = total


def weighted_kernel(terms_ref, misfit_ref, weight_ref, station_ref, place_ref, corr_ref, weighted_ref, out_ref):
    total = terms_ref[0]
    for s in range(1, terms_ref.shape[0]):
        total = total + terms_ref[s]
    hi_count = STATIONS // LANES
    corr = total[:hi_count] / (total[hi_count:] + 1.0)
    corr_ref[...] = corr
    stations = station_ref[...]
    high, low = stations >> 7, stations & (LANES - 1)
    table = jnp.concatenate(three_parts(corr), axis=0)
    found = []
    for r in range(stations.shape[0]):
        hot = pick(iota((LANES, LANES), 0) == low[r : r + 1])
        wide = jnp.dot(table, hot, preferred_element_type=F32)
        wide = (wide[:hi_count] + wide[hi_count : 2 * hi_count]) + wide[2 * hi_count :]
        own = iota((hi_count, LANES), 0) == high[r : r + 1]
        found.append(jnp.sum(jnp.where(own, wide, 0.0), axis=0, keepdims=True))
    weighted = weight_ref[...] * (misfit_ref[...] - jnp.concatenate(found, axis=0))
    weighted_ref[...] = weighted
    halves = jnp.concatenate(
        [weighted.astype(BF16), jnp.zeros((LANES - weighted.shape[0], LANES), BF16)], axis=0
    )
    lane = iota(place_ref.shape[1:], 1)
    half = (lane >= PICK_BLK).astype(jnp.int32)
    sent = None
    for h in (0, 1):
        place = place_ref[h]
        found = jnp.dot(pick(place >> 1 == lane), halves, preferred_element_type=F32)
        found = jnp.where((place & 1) == h, found, pltpu.roll(found, PICK_BLK, 1))
        sent = found if h == 0 else jnp.where(half == 0, sent, found)
    out_ref[...] = sent.astype(BF16).reshape(out_ref.shape)


def backward_kernel(code_ref, cell_ref, resid_ref, blocks_ref, out_ref, terms_ref):
    slots = blocks_ref.shape[0]
    lane, sub = iota((CHUNK, LANES), 1), iota((CHUNK, LANES), 0)
    sub_g = iota((GROUP, LANES), 0)
    parity = sub & 1
    half = (lane >= PICK_BLK).astype(jnp.int32)
    for n in range(slots // CHUNK):
        code_down = down(code_ref[n : n + 1, :])
        row_of = code_down >> 1
        chosen = jnp.concatenate(
            [pick(row_of == lane + t) for t in range(0, resid_ref.shape[0], LANES)], axis=1
        )
        resid = jnp.dot(chosen, resid_ref[...], preferred_element_type=F32)
        resid = jnp.where((code_down & 1) == parity, resid, pltpu.roll(resid, PICK_BLK, 1))
        resid = jnp.where(half == parity, resid, 0.0)
        parts = []
        for j in range(0, CHUNK, GROUP):
            block = blocks_ref[n * CHUNK + j : n * CHUNK + j + GROUP].reshape(GROUP * PICK_BLK, CELL_BLK)
            mine = resid[j : j + GROUP]
            wide = jnp.concatenate(
                [jnp.where(sub_g >> 1 == i, mine, 0.0) for i in range(GROUP // 2)], axis=1
            ).astype(BF16)
            parts.append(jnp.dot(wide, block, preferred_element_type=F32))
        high, low = two_parts(jnp.concatenate(parts, axis=0))
        terms_ref[n * CHUNK : (n + 1) * CHUNK, 0:LANES] = high
        terms_ref[n * CHUNK : (n + 1) * CHUNK, LANES : 2 * LANES] = low
    cells_of = cell_ref[...]
    both = terms_ref[...]
    tile = 2 * LANES
    for t in range(0, out_ref.shape[1], tile):
        hot = jnp.concatenate(
            [pick(iota((tile, LANES), 0) + t == cells_of[r : r + 1]) for r in range(slots // LANES)],
            axis=1,
        )
        sums = jnp.dot(hot, both, preferred_element_type=F32)
        sums = (sums[:, :LANES] + sums[:, LANES:]).astype(BF16)
        for s in range(out_ref.shape[0]):
            out_ref[s, t : t + tile, :] = sums


def gradient_kernel(terms_ref, out_ref):
    total = terms_ref[0].astype(F32)
    for s in range(1, terms_ref.shape[0]):
        total = total + terms_ref[s].astype(F32)
    out_ref[...] = total


def simple(kernel, out_shape, name, **more):
    return pl.pallas_call(
        kernel,
        out_shape=out_shape,
        compiler_params=pltpu.CompilerParams(vmem_limit_bytes=VMEM_BYTES),
        name=name,
        **more,
    )


def swap(x, axis, groups=None):
    return lax.all_to_all(x, axis, 0, 0, tiled=True, axis_index_groups=groups)


def torus_groups():
    lines, planes = {}, {}
    for x, zl, y, zh, c in itertools.product(range(4), range(2), range(4), range(4), range(2)):
        flat = (x * 2 + zl) * 32 + y * 8 + zh * 2 + c
        lines.setdefault((x, y), []).append(flat)
        planes.setdefault((zl, zh, c), []).append(flat)
    return list(lines.values()), list(planes.values())


def local(model, sensitivity, pick_block, cell_block, blk_count, observed, pick_weight, station):
    shells, events = lax.axis_size("shells"), lax.axis_size("events")
    picks_of = pick_block.reshape(-1, LANES)
    cells_of = cell_block.reshape(-1, LANES)
    model_rows = model.reshape(-1, CELL_BLK)
    observed, weight = observed.reshape(-1, LANES), pick_weight.reshape(-1, LANES)
    station = station.reshape(-1, LANES)
    own_rows = observed.shape[0]
    stat_rows = 2 * STATIONS // LANES
    shape = jax.ShapeDtypeStruct

    outside = pl.BlockSpec(memory_space=pltpu.HBM)
    lines, planes = torus_groups()
    devices = ("events", "shells")

    slots = sensitivity.shape[0]
    q = SLOT_CAP // 2
    partials, blocks, codes = pl.pallas_call(
        forward_kernel,
        in_specs=[outside] * 5,
        out_specs=(pl.BlockSpec(memory_space=pltpu.VMEM),) * 3,
        out_shape=(
            shape((shells, SLOT_CAP + 8, LANES), BF16),
            shape(sensitivity.shape, BF16),
            shape(picks_of.shape, jnp.int32),
        ),
        scratch_shapes=[
            pltpu.SMEM((1,), jnp.int32),
            pltpu.VMEM(picks_of.shape, jnp.int32),
            pltpu.VMEM(cells_of.shape, jnp.int32),
            pltpu.VMEM(model_rows.shape, BF16),
            pltpu.VMEM((slots, 2 * LANES), BF16),
            pltpu.VMEM((shells * q, slots), BF16),
            pltpu.SemaphoreType.DMA((4,)),
            pltpu.SemaphoreType.DMA((8,)),
        ],
        compiler_params=pltpu.CompilerParams(vmem_limit_bytes=VMEM_BYTES),
        name="forward",
    )(blk_count, picks_of, cells_of, model_rows, sensitivity)
    partials = swap(partials, "shells")
    misfit, places, stats = simple(
        stations_kernel,
        (
            shape((own_rows, LANES), F32),
            shape((2, shells * q, LANES), jnp.int32),
            shape((len(lines[0]), stat_rows, LANES), F32),
        ),
        "stations",
    )(partials, observed, weight, station)
    stats = swap(stats, devices, lines)
    stats = simple(spread_kernel, shape((len(planes[0]), stat_rows, LANES), F32), "spread")(stats)
    stats = swap(stats, devices, planes)
    correction, weighted, halves = simple(
        weighted_kernel,
        (
            shape((STATIONS // LANES, LANES), F32),
            shape((own_rows, LANES), F32),
            shape((shells, q, LANES), BF16),
        ),
        "weighted",
    )(stats, misfit, weight, station, places)
    halves = swap(halves, "shells").reshape(shells * q, LANES)
    grads = simple(
        backward_kernel,
        shape((events,) + model_rows.shape, BF16),
        "backward",
        scratch_shapes=[pltpu.VMEM((sensitivity.shape[0], 2 * LANES), BF16)],
    )(codes, cells_of, halves, blocks)
    grads = swap(grads, "events")
    gradient = simple(gradient_kernel, shape(model_rows.shape, F32), "gradient")(grads)
    return (gradient.reshape(-1), correction.reshape(-1), weighted.reshape(-1))


def solution(mesh):
    both = P(("events", "shells"))
    placed = (P("shells"), P(("events", "shells"), None, None)) + (both,) * 6
    return jax.shard_map(
        local,
        mesh=mesh,
        in_specs=placed,
        out_specs=(P("shells"), P(), both),
        check_vma=False,
    )
```

```python
import itertools

import jax
import jax.numpy as jnp
from jax import lax
from jax.experimental import pallas as pl
from jax.experimental.pallas import tpu as pltpu
from jax.sharding import PartitionSpec as P

PICK_BLK = 64
CELL_BLK = 128
STATIONS = 2048
LANES = 128
GROUP = 8
CHUNK = 128
F32 = jnp.float32
BF16 = jnp.bfloat16
NT = (((1,), (1,)), ((), ()))
TN = (((0,), (0,)), ((), ()))
SLOT_CAP = 32
VMEM_BYTES = 40 << 20


def iota(shape, axis):
    return lax.broadcasted_iota(jnp.int32, shape, axis)


def down(row):
    tall = jnp.broadcast_to(row.astype(F32), (LANES, LANES))
    return jnp.transpose(tall).astype(jnp.int32)


def pick(mask):
    return jnp.where(mask, 1.0, 0.0).astype(BF16)


def two_parts(x):
    high = x.astype(BF16)
    return high, (x - high.astype(F32)).astype(BF16)


def three_parts(x):
    high, rest = x.astype(BF16), x
    rest = x - high.astype(F32)
    mid = rest.astype(BF16)
    return high, mid, (rest - mid.astype(F32)).astype(BF16)


def forward_kernel(count_hbm, pick_hbm, cell_hbm, model_hbm, blocks_hbm, out_ref, blocks_ref, code_ref,
                   count, pick_ref, cell_ref, model_ref, values_ref, hot_ref, table_sems, block_sems):
    slots, cells = blocks_ref.shape[0], model_ref.shape[0]
    owners = out_ref.shape[0]
    chunks = range(slots // CHUNK)
    tables = [
        pltpu.make_async_copy(src, dst, table_sems.at[n])
        for n, (src, dst) in enumerate(
            [(count_hbm, count), (pick_hbm, pick_ref), (cell_hbm, cell_ref), (model_hbm, model_ref)]
        )
    ]
    for copy in tables:
        copy.start()
    copies = []
    piece = slots // block_sems.shape[0]
    for n in range(slots // piece):
        at = pl.ds(n * piece, piece)
        copies.append(pltpu.make_async_copy(blocks_hbm.at[at], blocks_ref.at[at], block_sems.at[n]))
        copies[-1].start()
    for copy in tables:
        copy.wait()
    lane, sub = iota((CHUNK, LANES), 1), iota((CHUNK, LANES), 0)
    half = (lane >= PICK_BLK).astype(jnp.int32)

    before, every = pick(sub < lane), jnp.ones((CHUNK, LANES), BF16)
    seen = jnp.zeros((owners, LANES), F32)
    index = jnp.zeros((owners * 8, LANES), F32)
    codes, code_down, rows = [], [], []
    for n in chunks:
        picks = pick_ref[n : n + 1, :]
        used = n * CHUNK + iota((1, LANES), 1) < count[0]
        owner, inside = picks >> 6, picks & (PICK_BLK - 1)
        mine = jnp.logical_and(iota((owners, LANES), 0) == owner, used)
        ones = pick(mine)
        ahead = seen + jnp.dot(ones, before, preferred_element_type=F32)
        seen = seen + jnp.dot(ones, every, preferred_element_type=F32)
        rank = jnp.sum(jnp.where(mine, ahead, 0.0), axis=0, keepdims=True).astype(jnp.int32)
        code = jnp.where(used, owner * SLOT_CAP + rank, -1)
        codes.append(code)
        code_ref[n : n + 1, :] = code
        code_down.append(down(code))
        cell_down = down(cell_ref[n : n + 1, :])
        chosen = jnp.concatenate([pick(cell_down == lane + t) for t in range(0, cells, LANES)], axis=1)
        rows.append(jnp.dot(chosen, model_ref[...], preferred_element_type=F32))
        tile_row = jnp.where(used, owner * 8 + ((code >> 1) & 7), -1)
        block = (inside & 1) * 32 + (inside >> 1) + 1
        tagged = iota((owners * 8, LANES), 0) == tile_row
        tagged = jnp.where(tagged, block.astype(F32), 0.0).astype(BF16)
        quarter = (code_down[n] & 1) * 2 + ((code_down[n] >> 4) & 1)
        index = index + jnp.dot(tagged, pick(lane >> 5 == quarter), preferred_element_type=F32)
        hot_ref[:, n * CHUNK : (n + 1) * CHUNK] = pick(iota((hot_ref.shape[0], LANES), 0) == code >> 1)
    out_ref[:, SLOT_CAP:, :] = index.astype(BF16).reshape(owners, 8, LANES)

    lane_g, sub_g = iota((GROUP, LANES), 1), iota((GROUP, LANES), 0)
    for n in chunks:
        parts = []
        for j in range(0, CHUNK, GROUP):
            first = n * CHUNK + j
            if first % piece == 0:
                copies[first // piece].wait()
            block = blocks_ref[first : first + GROUP].reshape(GROUP * PICK_BLK, CELL_BLK)
            wide = lax.dot_general(
                rows[n][j : j + GROUP].astype(BF16), block, NT, preferred_element_type=F32
            )
            part = jnp.zeros((GROUP, LANES), F32)
            for i in range(GROUP // 2):
                own = sub_g == 2 * i + (lane_g >= PICK_BLK).astype(jnp.int32)
                part = jnp.where(own, wide[:, i * LANES : (i + 1) * LANES], part)
            parts.append(part)
        values = jnp.concatenate(parts, axis=0)
        values = values + pltpu.roll(values, PICK_BLK, 1)
        values = jnp.where((code_down[n] & 1) == half, values, 0.0)
        high, low = two_parts(values)
        values_ref[n * CHUNK : (n + 1) * CHUNK, 0:LANES] = high
        values_ref[n * CHUNK : (n + 1) * CHUNK, LANES : 2 * LANES] = low
    placed = jnp.dot(hot_ref[...], values_ref[...], preferred_element_type=F32).astype(BF16)
    q = SLOT_CAP // 2
    out_ref[:, 0:q, :] = placed[:, :LANES].reshape(owners, q, LANES)
    out_ref[:, q : 2 * q, :] = placed[:, LANES:].reshape(owners, q, LANES)


def row_matches(terms_ref):
    tile = terms_ref[:, SLOT_CAP:, :].astype(F32).reshape(-1, LANES)
    lane = (iota(tile.shape, 1) & 31).astype(F32)
    return pick(tile == lane + 1.0), pick(tile == lane + 33.0)


def stations_kernel(terms_ref, observed_ref, weight_ref, station_ref, misfit_ref, out_ref):
    rows = observed_ref.shape[0]
    q = SLOT_CAP // 2

    def part(first):
        return terms_ref[:, first : first + 8, :].astype(F32).reshape(-1, LANES).astype(BF16)

    lower, upper = [jnp.concatenate([part(t), part(q + t)], axis=1) for t in (0, 8)]
    sides = []
    for match in row_matches(terms_ref):
        low_sum = lax.dot_general(match, lower, TN, preferred_element_type=F32)
        top_sum = lax.dot_general(match, upper, TN, preferred_element_type=F32)
        low_sum = low_sum[:, :LANES] + low_sum[:, LANES:]
        top_sum = top_sum[:, :LANES] + top_sum[:, LANES:]
        sides.append((low_sum[0:32] + top_sum[32:64], low_sum[64:96] + top_sum[96:128]))
    (even_left, even_right), (odd_left, odd_right) = sides
    predicted = jnp.where(
        iota((rows, LANES), 1) < PICK_BLK,
        even_left + pltpu.roll(even_right, PICK_BLK, 1),
        odd_right + pltpu.roll(odd_left, PICK_BLK, 1),
    )
    misfit = observed_ref[...] - predicted
    misfit_ref[...] = misfit
    weight = weight_ref[...]
    stations = station_ref[...]
    high, low = stations >> 7, stations & (LANES - 1)
    hi_count = STATIONS // LANES
    pieces = [p.astype(F32) for p in three_parts(weight * misfit) + three_parts(weight)]
    total = jnp.zeros((len(pieces) * hi_count, LANES), F32)
    for r0 in range(0, rows, 8):
        left, right = [], []
        for r in range(r0, r0 + 8):
            own = iota((hi_count, LANES), 0) == high[r : r + 1]
            left.append(
                jnp.concatenate([jnp.where(own, p[r : r + 1], 0.0) for p in pieces], axis=0).astype(BF16)
            )
            right.append(pick(iota((LANES, LANES), 0) == low[r : r + 1]))
        total = total + lax.dot_general(
            jnp.concatenate(left, axis=1), jnp.concatenate(right, axis=1), NT, preferred_element_type=F32
        )
    h = hi_count
    numer = total[0:h] + total[h : 2 * h] + total[2 * h : 3 * h]
    denom = total[3 * h : 4 * h] + total[4 * h : 5 * h] + total[5 * h : 6 * h]
    for s in range(out_ref.shape[0]):
        out_ref[s] = denom if s % 2 else numer


def spread_kernel(terms_ref, out_ref):
    total = terms_ref[0]
    for s in range(1, terms_ref.shape[0]):
        total = total + terms_ref[s]
    for s in range(out_ref.shape[0]):
        out_ref[s] = total


def weighted_kernel(terms_ref, misfit_ref, weight_ref, station_ref, partials_ref, corr_ref, weighted_ref, out_ref):
    numer, denom = terms_ref[0], terms_ref[1]
    for s in range(2, terms_ref.shape[0], 2):
        numer = numer + terms_ref[s]
        denom = denom + terms_ref[s + 1]
    corr = numer / (denom + 1.0)
    corr_ref[...] = corr
    stations = station_ref[...]
    high, low = stations >> 7, stations & (LANES - 1)
    found = jnp.zeros(stations.shape, F32)
    for h in range(corr.shape[0]):
        line = jnp.broadcast_to(corr[h : h + 1], stations.shape)
        found = jnp.where(high == h, jnp.take_along_axis(line, low, axis=1), found)
    weighted = weight_ref[...] * (misfit_ref[...] - found)
    weighted_ref[...] = weighted
    halves = weighted.astype(BF16).astype(F32)
    lane = iota(halves.shape, 1)
    left = lane < PICK_BLK
    turned = pltpu.roll(halves, PICK_BLK, 1)
    none = jnp.zeros_like(halves)
    tables = []
    for both in (jnp.where(left, halves, turned), jnp.where(left, turned, halves)):
        first, second = jnp.where(left, both, 0.0), jnp.where(left, 0.0, both)
        lower = jnp.concatenate([first, none, second, none], axis=0)
        upper = jnp.concatenate([none, first, none, second], axis=0)
        tables.append(jnp.concatenate([lower, upper], axis=1))
    table = jnp.concatenate(tables, axis=0).astype(BF16)
    matches = jnp.concatenate(row_matches(partials_ref), axis=1)
    sent = jnp.dot(matches, table, preferred_element_type=F32)
    peers = out_ref.shape[0]
    sent = [sent[:, t : t + LANES].reshape(peers, 8, LANES) for t in (0, LANES)]
    out_ref[...] = jnp.concatenate(sent, axis=1).astype(BF16)


def backward_kernel(code_ref, cell_ref, resid_ref, blocks_ref, out_ref, terms_ref):
    slots = blocks_ref.shape[0]
    lane, sub = iota((CHUNK, LANES), 1), iota((CHUNK, LANES), 0)
    sub_g = iota((GROUP, LANES), 0)
    parity = sub & 1
    half = (lane >= PICK_BLK).astype(jnp.int32)
    for n in range(slots // CHUNK):
        code_down = down(code_ref[n : n + 1, :])
        row_of = code_down >> 1
        chosen = jnp.concatenate(
            [pick(row_of == lane + t) for t in range(0, resid_ref.shape[0], LANES)], axis=1
        )
        resid = jnp.dot(chosen, resid_ref[...], preferred_element_type=F32)
        resid = jnp.where((code_down & 1) == parity, resid, pltpu.roll(resid, PICK_BLK, 1))
        resid = jnp.where(half == parity, resid, 0.0)
        parts = []
        for j in range(0, CHUNK, GROUP):
            block = blocks_ref[n * CHUNK + j : n * CHUNK + j + GROUP].reshape(GROUP * PICK_BLK, CELL_BLK)
            mine = resid[j : j + GROUP]
            wide = jnp.concatenate(
                [jnp.where(sub_g >> 1 == i, mine, 0.0) for i in range(GROUP // 2)], axis=1
            ).astype(BF16)
            parts.append(jnp.dot(wide, block, preferred_element_type=F32))
        high, low = two_parts(jnp.concatenate(parts, axis=0))
        terms_ref[n * CHUNK : (n + 1) * CHUNK, 0:LANES] = high
        terms_ref[n * CHUNK : (n + 1) * CHUNK, LANES : 2 * LANES] = low
    cells_of = cell_ref[...]
    both = terms_ref[...]
    tile = 2 * LANES
    for t in range(0, out_ref.shape[1], tile):
        hot = jnp.concatenate(
            [pick(iota((tile, LANES), 0) + t == cells_of[r : r + 1]) for r in range(slots // LANES)],
            axis=1,
        )
        sums = jnp.dot(hot, both, preferred_element_type=F32)
        sums = (sums[:, :LANES] + sums[:, LANES:]).astype(BF16)
        for s in range(out_ref.shape[0]):
            out_ref[s, t : t + tile, :] = sums


def gradient_kernel(terms_ref, out_hbm, total_ref, sems):
    pieces = sems.shape[0]
    rows = total_ref.shape[0] // pieces
    copies = []
    for n in range(pieces):
        at = pl.ds(n * rows, rows)
        total = terms_ref[0, at, :].astype(F32)
        for s in range(1, terms_ref.shape[0]):
            total = total + terms_ref[s, at, :].astype(F32)
        total_ref[at, :] = total
        copies.append(pltpu.make_async_copy(total_ref.at[at], out_hbm.at[at], sems.at[n]))
        copies[-1].start()
    for copy in copies:
        copy.wait()


def simple(kernel, out_shape, name, **more):
    return pl.pallas_call(
        kernel,
        out_shape=out_shape,
        compiler_params=pltpu.CompilerParams(vmem_limit_bytes=VMEM_BYTES),
        name=name,
        **more,
    )


def swap(x, axis, groups=None):
    return lax.all_to_all(x, axis, 0, 0, tiled=True, axis_index_groups=groups)


def torus_groups():
    lines, planes = {}, {}
    for x, zl, y, zh, c in itertools.product(range(4), range(2), range(4), range(4), range(2)):
        flat = (x * 2 + zl) * 32 + y * 8 + zh * 2 + c
        lines.setdefault((x, y), []).append(flat)
        planes.setdefault((zl, zh), []).append(flat)
    return list(lines.values()), list(planes.values())


def local(model, sensitivity, pick_block, cell_block, blk_count, observed, pick_weight, station):
    shells, events = lax.axis_size("shells"), lax.axis_size("events")
    picks_of = pick_block.reshape(-1, LANES)
    cells_of = cell_block.reshape(-1, LANES)
    model_rows = model.reshape(-1, CELL_BLK)
    observed, weight = observed.reshape(-1, LANES), pick_weight.reshape(-1, LANES)
    station = station.reshape(-1, LANES)
    own_rows = observed.shape[0]
    stat_rows = STATIONS // LANES
    shape = jax.ShapeDtypeStruct

    outside = pl.BlockSpec(memory_space=pltpu.HBM)
    lines, planes = torus_groups()
    devices = ("events", "shells")

    slots = sensitivity.shape[0]
    q = SLOT_CAP // 2
    partials, blocks, codes = pl.pallas_call(
        forward_kernel,
        in_specs=[outside] * 5,
        out_specs=(pl.BlockSpec(memory_space=pltpu.VMEM),) * 3,
        out_shape=(
            shape((shells, SLOT_CAP + 8, LANES), BF16),
            shape(sensitivity.shape, BF16),
            shape(picks_of.shape, jnp.int32),
        ),
        scratch_shapes=[
            pltpu.SMEM((1,), jnp.int32),
            pltpu.VMEM(picks_of.shape, jnp.int32),
            pltpu.VMEM(cells_of.shape, jnp.int32),
            pltpu.VMEM(model_rows.shape, BF16),
            pltpu.VMEM((slots, 2 * LANES), BF16),
            pltpu.VMEM((shells * q, slots), BF16),
            pltpu.SemaphoreType.DMA((4,)),
            pltpu.SemaphoreType.DMA((8,)),
        ],
        compiler_params=pltpu.CompilerParams(vmem_limit_bytes=VMEM_BYTES),
        name="forward",
    )(
        blk_count,
        *[
            pltpu.with_memory_space_constraint(v, pltpu.HBM)
            for v in (picks_of, cells_of, model_rows, sensitivity)
        ],
    )
    partials = swap(partials, "shells")
    misfit, stats = simple(
        stations_kernel,
        (
            shape((own_rows, LANES), F32),
            shape((len(lines[0]), stat_rows, LANES), F32),
        ),
        "stations",
    )(partials, observed, weight, station)
    stats = swap(stats, devices, lines)
    stats = simple(spread_kernel, shape((len(planes[0]), stat_rows, LANES), F32), "spread")(stats)
    stats = swap(stats, devices, planes)
    correction, weighted, halves = simple(
        weighted_kernel,
        (
            shape((STATIONS // LANES, LANES), F32),
            shape((own_rows, LANES), F32),
            shape((shells, q, LANES), BF16),
        ),
        "weighted",
    )(stats, misfit, weight, station, partials)
    halves = swap(halves, "shells").reshape(shells * q, LANES)
    grads = simple(
        backward_kernel,
        shape((events,) + model_rows.shape, BF16),
        "backward",
        scratch_shapes=[pltpu.VMEM((sensitivity.shape[0], 2 * LANES), BF16)],
    )(codes, cells_of, halves, blocks)
    grads = swap(grads, "events")
    gradient = simple(
        gradient_kernel,
        shape(model_rows.shape, F32),
        "gradient",
        out_specs=outside,
        scratch_shapes=[pltpu.VMEM(model_rows.shape, F32), pltpu.SemaphoreType.DMA((4,))],
    )(grads)
    return (gradient.reshape(-1), correction.reshape(-1), weighted.reshape(-1))


def solution(mesh):
    both = P(("events", "shells"))
    placed = (P("shells"), P(("events", "shells"), None, None)) + (both,) * 6
    return jax.shard_map(
        local,
        mesh=mesh,
        in_specs=placed,
        out_specs=(P("shells"), P(), both),
        check_vma=False,
    )
```

```python
import itertools

import jax
import jax.numpy as jnp
from jax import lax
from jax.experimental import pallas as pl
from jax.experimental.pallas import tpu as pltpu
from jax.sharding import PartitionSpec as P

PICK_BLK = 64
CELL_BLK = 128
STATIONS = 2048
LANES = 128
GROUP = 8
CHUNK = 128
F32 = jnp.float32
BF16 = jnp.bfloat16
NT = (((1,), (1,)), ((), ()))
TN = (((0,), (0,)), ((), ()))
SLOT_CAP = 32
VMEM_BYTES = 40 << 20


def iota(shape, axis):
    return lax.broadcasted_iota(jnp.int32, shape, axis)


def down(row):
    tall = jnp.broadcast_to(row.astype(F32), (LANES, LANES))
    return jnp.transpose(tall).astype(jnp.int32)


def pick(mask):
    return jnp.where(mask, 1.0, 0.0).astype(BF16)


def two_parts(x):
    high = x.astype(BF16)
    return high, (x - high.astype(F32)).astype(BF16)


def three_parts(x):
    high, rest = x.astype(BF16), x
    rest = x - high.astype(F32)
    mid = rest.astype(BF16)
    return high, mid, (rest - mid.astype(F32)).astype(BF16)


def forward_kernel(count_hbm, pick_hbm, cell_hbm, model_hbm, blocks_hbm, out_ref, blocks_ref, code_ref,
                   count, pick_ref, cell_ref, model_ref, values_ref, hot_ref, table_sems, block_sems):
    slots, cells = blocks_ref.shape[0], model_ref.shape[0]
    owners = out_ref.shape[0]
    chunks = range(slots // CHUNK)
    tables = [
        pltpu.make_async_copy(src, dst, table_sems.at[n])
        for n, (src, dst) in enumerate(
            [(count_hbm, count), (pick_hbm, pick_ref), (cell_hbm, cell_ref), (model_hbm, model_ref)]
        )
    ]
    for copy in tables:
        copy.start()
    piece = slots // block_sems.shape[0]

    def block_copy(n):
        at = pl.ds(n * piece, piece)
        return pltpu.make_async_copy(blocks_hbm.at[at], blocks_ref.at[at], block_sems.at[n])

    def start_copy(n, carry):
        block_copy(n).start()
        return carry

    lax.fori_loop(0, slots // piece, start_copy, 0)
    for copy in tables:
        copy.wait()
    lane, sub = iota((CHUNK, LANES), 1), iota((CHUNK, LANES), 0)
    half = (lane >= PICK_BLK).astype(jnp.int32)

    before, every = pick(sub < lane), jnp.ones((CHUNK, LANES), BF16)
    seen = jnp.zeros((owners, LANES), F32)
    index = jnp.zeros((owners * 8, LANES), F32)
    codes, code_down, rows = [], [], []
    for n in chunks:
        picks = pick_ref[n : n + 1, :]
        used = n * CHUNK + iota((1, LANES), 1) < count[0]
        owner, inside = picks >> 6, picks & (PICK_BLK - 1)
        mine = jnp.logical_and(iota((owners, LANES), 0) == owner, used)
        ones = pick(mine)
        ahead = seen + jnp.dot(ones, before, preferred_element_type=F32)
        seen = seen + jnp.dot(ones, every, preferred_element_type=F32)
        rank = jnp.sum(jnp.where(mine, ahead, 0.0), axis=0, keepdims=True).astype(jnp.int32)
        code = jnp.where(used, owner * SLOT_CAP + rank, -1)
        codes.append(code)
        code_ref[n : n + 1, :] = code
        code_down.append(down(code))
        cell_down = down(cell_ref[n : n + 1, :])
        chosen = jnp.concatenate([pick(cell_down == lane + t) for t in range(0, cells, LANES)], axis=1)
        rows.append(jnp.dot(chosen, model_ref[...], preferred_element_type=F32))
        tile_row = jnp.where(used, owner * 8 + ((code >> 1) & 7), -1)
        block = (inside & 1) * 32 + (inside >> 1) + 1
        tagged = iota((owners * 8, LANES), 0) == tile_row
        tagged = jnp.where(tagged, block.astype(F32), 0.0).astype(BF16)
        quarter = (code_down[n] & 1) * 2 + ((code_down[n] >> 4) & 1)
        index = index + jnp.dot(tagged, pick(lane >> 5 == quarter), preferred_element_type=F32)
        hot_ref[:, n * CHUNK : (n + 1) * CHUNK] = pick(iota((hot_ref.shape[0], LANES), 0) == code >> 1)
    out_ref[:, SLOT_CAP:, :] = index.astype(BF16).reshape(owners, 8, LANES)

    lane_g, sub_g = iota((GROUP, LANES), 1), iota((GROUP, LANES), 0)
    for n in chunks:
        parts = []
        for j in range(0, CHUNK, GROUP):
            first = n * CHUNK + j
            if first % piece == 0:
                block_copy(first // piece).wait()
            block = blocks_ref[first : first + GROUP].reshape(GROUP * PICK_BLK, CELL_BLK)
            wide = lax.dot_general(
                rows[n][j : j + GROUP].astype(BF16), block, NT, preferred_element_type=F32
            )
            part = jnp.zeros((GROUP, LANES), F32)
            for i in range(GROUP // 2):
                own = sub_g == 2 * i + (lane_g >= PICK_BLK).astype(jnp.int32)
                part = jnp.where(own, wide[:, i * LANES : (i + 1) * LANES], part)
            parts.append(part)
        values = jnp.concatenate(parts, axis=0)
        values = values + pltpu.roll(values, PICK_BLK, 1)
        values = jnp.where((code_down[n] & 1) == half, values, 0.0)
        high, low = two_parts(values)
        values_ref[n * CHUNK : (n + 1) * CHUNK, 0:LANES] = high
        values_ref[n * CHUNK : (n + 1) * CHUNK, LANES : 2 * LANES] = low
    placed = jnp.dot(hot_ref[...], values_ref[...], preferred_element_type=F32).astype(BF16)
    q = SLOT_CAP // 2
    out_ref[:, 0:q, :] = placed[:, :LANES].reshape(owners, q, LANES)
    out_ref[:, q : 2 * q, :] = placed[:, LANES:].reshape(owners, q, LANES)


def row_matches(terms_ref):
    tile = terms_ref[:, SLOT_CAP:, :].astype(F32).reshape(-1, LANES)
    lane = (iota(tile.shape, 1) & 31).astype(F32)
    return pick(tile == lane + 1.0), pick(tile == lane + 33.0)


def stations_kernel(terms_ref, observed_ref, weight_ref, station_ref, misfit_ref, out_ref):
    rows = observed_ref.shape[0]
    q = SLOT_CAP // 2

    def part(first):
        return terms_ref[:, first : first + 8, :].astype(F32).reshape(-1, LANES).astype(BF16)

    lower, upper = [jnp.concatenate([part(t), part(q + t)], axis=1) for t in (0, 8)]
    sides = []
    for match in row_matches(terms_ref):
        low_sum = lax.dot_general(match, lower, TN, preferred_element_type=F32)
        top_sum = lax.dot_general(match, upper, TN, preferred_element_type=F32)
        low_sum = low_sum[:, :LANES] + low_sum[:, LANES:]
        top_sum = top_sum[:, :LANES] + top_sum[:, LANES:]
        sides.append((low_sum[0:32] + top_sum[32:64], low_sum[64:96] + top_sum[96:128]))
    (even_left, even_right), (odd_left, odd_right) = sides
    predicted = jnp.where(
        iota((rows, LANES), 1) < PICK_BLK,
        even_left + pltpu.roll(even_right, PICK_BLK, 1),
        odd_right + pltpu.roll(odd_left, PICK_BLK, 1),
    )
    misfit = observed_ref[...] - predicted
    misfit_ref[...] = misfit
    weight = weight_ref[...]
    stations = station_ref[...]
    high, low = stations >> 7, stations & (LANES - 1)
    hi_count = STATIONS // LANES
    pieces = [p.astype(F32) for p in three_parts(weight * misfit) + three_parts(weight)]
    total = jnp.zeros((len(pieces) * hi_count, LANES), F32)
    for r0 in range(0, rows, 8):
        left, right = [], []
        for r in range(r0, r0 + 8):
            own = iota((hi_count, LANES), 0) == high[r : r + 1]
            left.append(
                jnp.concatenate([jnp.where(own, p[r : r + 1], 0.0) for p in pieces], axis=0).astype(BF16)
            )
            right.append(pick(iota((LANES, LANES), 0) == low[r : r + 1]))
        total = total + lax.dot_general(
            jnp.concatenate(left, axis=1), jnp.concatenate(right, axis=1), NT, preferred_element_type=F32
        )
    h = hi_count
    numer = total[0:h] + total[h : 2 * h] + total[2 * h : 3 * h]
    denom = total[3 * h : 4 * h] + total[4 * h : 5 * h] + total[5 * h : 6 * h]
    for s in range(out_ref.shape[0]):
        out_ref[s] = denom if s % 2 else numer


def spread_kernel(terms_ref, out_ref):
    total = terms_ref[0]
    for s in range(1, terms_ref.shape[0]):
        total = total + terms_ref[s]
    for s in range(out_ref.shape[0]):
        out_ref[s] = total


def weighted_kernel(terms_ref, misfit_ref, weight_ref, station_ref, partials_ref, corr_ref, weighted_ref, out_ref):
    numer, denom = terms_ref[0], terms_ref[1]
    for s in range(2, terms_ref.shape[0], 2):
        numer = numer + terms_ref[s]
        denom = denom + terms_ref[s + 1]
    corr = numer / (denom + 1.0)
    corr_ref[...] = corr
    stations = station_ref[...]
    high, low = stations >> 7, stations & (LANES - 1)
    found = jnp.zeros(stations.shape, F32)
    for h in range(corr.shape[0]):
        line = jnp.broadcast_to(corr[h : h + 1], stations.shape)
        found = jnp.where(high == h, jnp.take_along_axis(line, low, axis=1), found)
    weighted = weight_ref[...] * (misfit_ref[...] - found)
    weighted_ref[...] = weighted
    halves = weighted.astype(BF16).astype(F32)
    lane = iota(halves.shape, 1)
    left = lane < PICK_BLK
    turned = pltpu.roll(halves, PICK_BLK, 1)
    none = jnp.zeros_like(halves)
    tables = []
    for both in (jnp.where(left, halves, turned), jnp.where(left, turned, halves)):
        first, second = jnp.where(left, both, 0.0), jnp.where(left, 0.0, both)
        lower = jnp.concatenate([first, none, second, none], axis=0)
        upper = jnp.concatenate([none, first, none, second], axis=0)
        tables.append(jnp.concatenate([lower, upper], axis=1))
    table = jnp.concatenate(tables, axis=0).astype(BF16)
    matches = jnp.concatenate(row_matches(partials_ref), axis=1)
    sent = jnp.dot(matches, table, preferred_element_type=F32)
    peers = out_ref.shape[0]
    sent = [sent[:, t : t + LANES].reshape(peers, 8, LANES) for t in (0, LANES)]
    out_ref[...] = jnp.concatenate(sent, axis=1).astype(BF16)


def backward_kernel(code_ref, cell_ref, resid_ref, blocks_ref, corr_ref, weighted_ref,
                    out_ref, corr_hbm, weighted_hbm, terms_ref, sems):
    copies = [
        pltpu.make_async_copy(corr_ref, corr_hbm, sems.at[0]),
        pltpu.make_async_copy(weighted_ref, weighted_hbm, sems.at[1]),
    ]
    for copy in copies:
        copy.start()
    slots = blocks_ref.shape[0]
    lane, sub = iota((CHUNK, LANES), 1), iota((CHUNK, LANES), 0)
    sub_g = iota((GROUP, LANES), 0)
    parity = sub & 1
    half = (lane >= PICK_BLK).astype(jnp.int32)
    for n in range(slots // CHUNK):
        code_down = down(code_ref[n : n + 1, :])
        row_of = code_down >> 1
        chosen = jnp.concatenate(
            [pick(row_of == lane + t) for t in range(0, resid_ref.shape[0], LANES)], axis=1
        )
        resid = jnp.dot(chosen, resid_ref[...], preferred_element_type=F32)
        resid = jnp.where((code_down & 1) == parity, resid, pltpu.roll(resid, PICK_BLK, 1))
        resid = jnp.where(half == parity, resid, 0.0)
        parts = []
        for j in range(0, CHUNK, GROUP):
            block = blocks_ref[n * CHUNK + j : n * CHUNK + j + GROUP].reshape(GROUP * PICK_BLK, CELL_BLK)
            mine = resid[j : j + GROUP]
            wide = jnp.concatenate(
                [jnp.where(sub_g >> 1 == i, mine, 0.0) for i in range(GROUP // 2)], axis=1
            ).astype(BF16)
            parts.append(jnp.dot(wide, block, preferred_element_type=F32))
        high, low = two_parts(jnp.concatenate(parts, axis=0))
        terms_ref[n * CHUNK : (n + 1) * CHUNK, 0:LANES] = high
        terms_ref[n * CHUNK : (n + 1) * CHUNK, LANES : 2 * LANES] = low
    cells_of = cell_ref[...]
    both = terms_ref[...]
    tile = 2 * LANES
    for t in range(0, out_ref.shape[1], tile):
        hot = jnp.concatenate(
            [pick(iota((tile, LANES), 0) + t == cells_of[r : r + 1]) for r in range(slots // LANES)],
            axis=1,
        )
        sums = jnp.dot(hot, both, preferred_element_type=F32)
        sums = (sums[:, :LANES] + sums[:, LANES:]).astype(BF16)
        for s in range(out_ref.shape[0]):
            out_ref[s, t : t + tile, :] = sums
    for copy in copies:
        copy.wait()


def gradient_kernel(terms_ref, out_hbm, total_ref, sems):
    pieces = sems.shape[0]
    rows = total_ref.shape[0] // pieces
    copies = []
    for n in range(pieces):
        at = pl.ds(n * rows, rows)
        total = terms_ref[0, at, :].astype(F32)
        for s in range(1, terms_ref.shape[0]):
            total = total + terms_ref[s, at, :].astype(F32)
        total_ref[at, :] = total
        copies.append(pltpu.make_async_copy(total_ref.at[at], out_hbm.at[at], sems.at[n]))
        copies[-1].start()
    for copy in copies:
        copy.wait()


def simple(kernel, out_shape, name, **more):
    return pl.pallas_call(
        kernel,
        out_shape=out_shape,
        compiler_params=pltpu.CompilerParams(vmem_limit_bytes=VMEM_BYTES),
        name=name,
        **more,
    )


def swap(x, axis, groups=None):
    return lax.all_to_all(x, axis, 0, 0, tiled=True, axis_index_groups=groups)


def torus_groups():
    lines, planes = {}, {}
    for x, zl, y, zh, c in itertools.product(range(4), range(2), range(4), range(4), range(2)):
        flat = (x * 2 + zl) * 32 + y * 8 + zh * 2 + c
        lines.setdefault((x, y), []).append(flat)
        planes.setdefault((zl, zh), []).append(flat)
    return list(lines.values()), list(planes.values())


def local(model, sensitivity, pick_block, cell_block, blk_count, observed, pick_weight, station):
    shells, events = lax.axis_size("shells"), lax.axis_size("events")
    picks_of = pick_block.reshape(-1, LANES)
    cells_of = cell_block.reshape(-1, LANES)
    model_rows = model.reshape(-1, CELL_BLK)
    observed, weight = observed.reshape(-1, LANES), pick_weight.reshape(-1, LANES)
    station = station.reshape(-1, LANES)
    own_rows = observed.shape[0]
    stat_rows = STATIONS // LANES
    shape = jax.ShapeDtypeStruct

    outside = pl.BlockSpec(memory_space=pltpu.HBM)
    lines, planes = torus_groups()
    devices = ("events", "shells")

    slots = sensitivity.shape[0]
    q = SLOT_CAP // 2
    partials, blocks, codes = pl.pallas_call(
        forward_kernel,
        in_specs=[outside] * 5,
        out_specs=(pl.BlockSpec(memory_space=pltpu.VMEM),) * 3,
        out_shape=(
            shape((shells, SLOT_CAP + 8, LANES), BF16),
            shape(sensitivity.shape, BF16),
            shape(picks_of.shape, jnp.int32),
        ),
        scratch_shapes=[
            pltpu.SMEM((1,), jnp.int32),
            pltpu.VMEM(picks_of.shape, jnp.int32),
            pltpu.VMEM(cells_of.shape, jnp.int32),
            pltpu.VMEM(model_rows.shape, BF16),
            pltpu.VMEM((slots, 2 * LANES), BF16),
            pltpu.VMEM((shells * q, slots), BF16),
            pltpu.SemaphoreType.DMA((4,)),
            pltpu.SemaphoreType.DMA((16,)),
        ],
        compiler_params=pltpu.CompilerParams(vmem_limit_bytes=VMEM_BYTES),
        name="forward",
    )(
        blk_count,
        *[
            pltpu.with_memory_space_constraint(v, pltpu.HBM)
            for v in (picks_of, cells_of, model_rows, sensitivity)
        ],
    )
    partials = swap(partials, "shells")
    misfit, stats = simple(
        stations_kernel,
        (
            shape((own_rows, LANES), F32),
            shape((len(lines[0]), stat_rows, LANES), F32),
        ),
        "stations",
    )(partials, observed, weight, station)
    stats = swap(stats, devices, lines)
    stats = simple(spread_kernel, shape((len(planes[0]), stat_rows, LANES), F32), "spread")(stats)
    stats = swap(stats, devices, planes)
    correction, weighted, halves = simple(
        weighted_kernel,
        (
            shape((STATIONS // LANES, LANES), F32),
            shape((own_rows, LANES), F32),
            shape((shells, q, LANES), BF16),
        ),
        "weighted",
    )(stats, misfit, weight, station, partials)
    halves = swap(halves, "shells").reshape(shells * q, LANES)
    vmem = pl.BlockSpec(memory_space=pltpu.VMEM)
    grads, correction, weighted = simple(
        backward_kernel,
        (
            shape((events,) + model_rows.shape, BF16),
            shape(correction.shape, F32),
            shape(weighted.shape, F32),
        ),
        "backward",
        out_specs=(vmem, outside, outside),
        scratch_shapes=[pltpu.VMEM((slots, 2 * LANES), BF16), pltpu.SemaphoreType.DMA((2,))],
    )(codes, cells_of, halves, blocks, correction, weighted)
    grads = swap(grads, "events")
    gradient = simple(
        gradient_kernel,
        shape(model_rows.shape, F32),
        "gradient",
        out_specs=outside,
        scratch_shapes=[pltpu.VMEM(model_rows.shape, F32), pltpu.SemaphoreType.DMA((4,))],
    )(grads)
    return (gradient.reshape(-1), correction.reshape(-1), weighted.reshape(-1))


def solution(mesh):
    both = P(("events", "shells"))
    placed = (P("shells"), P(("events", "shells"), None, None)) + (both,) * 6
    return jax.shard_map(
        local,
        mesh=mesh,
        in_specs=placed,
        out_specs=(P("shells"), P(), both),
        check_vma=False,
    )
```

```python
import itertools

import jax
import jax.numpy as jnp
from jax import lax
from jax.experimental import pallas as pl
from jax.experimental.pallas import tpu as pltpu
from jax.sharding import PartitionSpec as P

PICK_BLK = 64
CELL_BLK = 128
STATIONS = 2048
LANES = 128
GROUP = 8
CHUNK = 128
F32 = jnp.float32
BF16 = jnp.bfloat16
NT = (((1,), (1,)), ((), ()))
TN = (((0,), (0,)), ((), ()))
SLOT_CAP = 32
VMEM_BYTES = 40 << 20
OUTSIDE = pl.BlockSpec(memory_space=pltpu.HBM)
INSIDE = pl.BlockSpec(memory_space=pltpu.VMEM)


def iota(shape, axis):
    return lax.broadcasted_iota(jnp.int32, shape, axis)


def down(row):
    tall = jnp.broadcast_to(row.astype(F32), (LANES, LANES))
    return jnp.transpose(tall).astype(jnp.int32)


def pick(mask):
    return jnp.where(mask, 1.0, 0.0).astype(BF16)


def two_parts(x):
    high = x.astype(BF16)
    return high, (x - high.astype(F32)).astype(BF16)


def three_parts(x):
    high, rest = x.astype(BF16), x
    rest = x - high.astype(F32)
    mid = rest.astype(BF16)
    return high, mid, (rest - mid.astype(F32)).astype(BF16)


def forward_kernel(count_hbm, pick_hbm, cell_hbm, model_hbm, blocks_hbm, out_ref, blocks_ref, code_ref,
                   count, pick_ref, cell_ref, model_ref, values_ref, hot_ref, table_sems, block_sem):
    slots, cells = blocks_ref.shape[0], model_ref.shape[0]
    owners = out_ref.shape[0]
    chunks = range(slots // CHUNK)
    tables = [
        pltpu.make_async_copy(src, dst, table_sems.at[n])
        for n, (src, dst) in enumerate(
            [(count_hbm, count), (pick_hbm, pick_ref), (cell_hbm, cell_ref), (model_hbm, model_ref)]
        )
    ]
    for copy in tables:
        copy.start()
    block_copy = pltpu.make_async_copy(blocks_hbm, blocks_ref, block_sem)
    block_copy.start()
    for copy in tables:
        copy.wait()
    lane, sub = iota((CHUNK, LANES), 1), iota((CHUNK, LANES), 0)
    half = (lane >= PICK_BLK).astype(jnp.int32)

    before, every = pick(sub < lane), jnp.ones((CHUNK, LANES), BF16)
    seen = jnp.zeros((owners, LANES), F32)
    index = jnp.zeros((owners * 8, LANES), F32)
    codes, code_down, rows = [], [], []
    for n in chunks:
        picks = pick_ref[n : n + 1, :]
        used = n * CHUNK + iota((1, LANES), 1) < count[0]
        owner, inside = picks >> 6, picks & (PICK_BLK - 1)
        mine = jnp.logical_and(iota((owners, LANES), 0) == owner, used)
        ones = pick(mine)
        ahead = seen + jnp.dot(ones, before, preferred_element_type=F32)
        seen = seen + jnp.dot(ones, every, preferred_element_type=F32)
        rank = jnp.sum(jnp.where(mine, ahead, 0.0), axis=0, keepdims=True).astype(jnp.int32)
        code = jnp.where(used, owner * SLOT_CAP + rank, -1)
        codes.append(code)
        code_ref[n : n + 1, :] = code
        code_down.append(down(code))
        cell_down = down(cell_ref[n : n + 1, :])
        chosen = jnp.concatenate([pick(cell_down == lane + t) for t in range(0, cells, LANES)], axis=1)
        rows.append(jnp.dot(chosen, model_ref[...], preferred_element_type=F32))
        tile_row = jnp.where(used, owner * 8 + ((code >> 1) & 7), -1)
        block = (inside & 1) * 32 + (inside >> 1) + 1
        tagged = iota((owners * 8, LANES), 0) == tile_row
        tagged = jnp.where(tagged, block.astype(F32), 0.0).astype(BF16)
        quarter = (code_down[n] & 1) * 2 + ((code_down[n] >> 4) & 1)
        index = index + jnp.dot(tagged, pick(lane >> 5 == quarter), preferred_element_type=F32)
        hot_ref[:, n * CHUNK : (n + 1) * CHUNK] = pick(iota((hot_ref.shape[0], LANES), 0) == code >> 1)
    out_ref[:, SLOT_CAP:, :] = index.astype(BF16).reshape(owners, 8, LANES)

    lane_g, sub_g = iota((GROUP, LANES), 1), iota((GROUP, LANES), 0)
    block_copy.wait()
    for n in chunks:
        parts = []
        for j in range(0, CHUNK, GROUP):
            first = n * CHUNK + j
            block = blocks_ref[first : first + GROUP].reshape(GROUP * PICK_BLK, CELL_BLK)
            wide = lax.dot_general(
                rows[n][j : j + GROUP].astype(BF16), block, NT, preferred_element_type=F32
            )
            part = jnp.zeros((GROUP, LANES), F32)
            for i in range(GROUP // 2):
                own = sub_g == 2 * i + (lane_g >= PICK_BLK).astype(jnp.int32)
                part = jnp.where(own, wide[:, i * LANES : (i + 1) * LANES], part)
            parts.append(part)
        values = jnp.concatenate(parts, axis=0)
        values = values + pltpu.roll(values, PICK_BLK, 1)
        values = jnp.where((code_down[n] & 1) == half, values, 0.0)
        high, low = two_parts(values)
        values_ref[n * CHUNK : (n + 1) * CHUNK, 0:LANES] = high
        values_ref[n * CHUNK : (n + 1) * CHUNK, LANES : 2 * LANES] = low
    placed = jnp.dot(hot_ref[...], values_ref[...], preferred_element_type=F32).astype(BF16)
    q = SLOT_CAP // 2
    out_ref[:, 0:q, :] = placed[:, :LANES].reshape(owners, q, LANES)
    out_ref[:, q : 2 * q, :] = placed[:, LANES:].reshape(owners, q, LANES)


def row_matches(terms_ref):
    tile = terms_ref[:, SLOT_CAP:, :].astype(F32).reshape(-1, LANES)
    lane = (iota(tile.shape, 1) & 31).astype(F32)
    return pick(tile == lane + 1.0), pick(tile == lane + 33.0)


def stations_kernel(terms_ref, observed_ref, weight_ref, station_ref, misfit_ref, out_ref):
    rows = observed_ref.shape[0]
    q = SLOT_CAP // 2

    def part(first):
        return terms_ref[:, first : first + 8, :].astype(F32).reshape(-1, LANES).astype(BF16)

    lower, upper = [jnp.concatenate([part(t), part(q + t)], axis=1) for t in (0, 8)]
    sides = []
    for match in row_matches(terms_ref):
        low_sum = lax.dot_general(match, lower, TN, preferred_element_type=F32)
        top_sum = lax.dot_general(match, upper, TN, preferred_element_type=F32)
        low_sum = low_sum[:, :LANES] + low_sum[:, LANES:]
        top_sum = top_sum[:, :LANES] + top_sum[:, LANES:]
        sides.append((low_sum[0:32] + top_sum[32:64], low_sum[64:96] + top_sum[96:128]))
    (even_left, even_right), (odd_left, odd_right) = sides
    predicted = jnp.where(
        iota((rows, LANES), 1) < PICK_BLK,
        even_left + pltpu.roll(even_right, PICK_BLK, 1),
        odd_right + pltpu.roll(odd_left, PICK_BLK, 1),
    )
    misfit = observed_ref[...] - predicted
    misfit_ref[...] = misfit
    weight = weight_ref[...]
    stations = station_ref[...]
    high, low = stations >> 7, stations & (LANES - 1)
    hi_count = STATIONS // LANES
    pieces = [p.astype(F32) for p in three_parts(weight * misfit) + three_parts(weight)]
    total = jnp.zeros((len(pieces) * hi_count, LANES), F32)
    for r0 in range(0, rows, 8):
        left, right = [], []
        for r in range(r0, r0 + 8):
            own = iota((hi_count, LANES), 0) == high[r : r + 1]
            left.append(
                jnp.concatenate([jnp.where(own, p[r : r + 1], 0.0) for p in pieces], axis=0).astype(BF16)
            )
            right.append(pick(iota((LANES, LANES), 0) == low[r : r + 1]))
        total = total + lax.dot_general(
            jnp.concatenate(left, axis=1), jnp.concatenate(right, axis=1), NT, preferred_element_type=F32
        )
    h = hi_count
    numer = total[0:h] + total[h : 2 * h] + total[2 * h : 3 * h]
    denom = total[3 * h : 4 * h] + total[4 * h : 5 * h] + total[5 * h : 6 * h]
    for s in range(out_ref.shape[0]):
        out_ref[s] = denom if s % 2 else numer


def spread_kernel(terms_ref, out_ref):
    total = terms_ref[0]
    for s in range(1, terms_ref.shape[0]):
        total = total + terms_ref[s]
    for s in range(out_ref.shape[0]):
        out_ref[s] = total


def weighted_kernel(terms_ref, misfit_ref, weight_ref, station_ref, partials_ref, corr_ref, weighted_ref, out_ref):
    numer, denom = terms_ref[0], terms_ref[1]
    for s in range(2, terms_ref.shape[0], 2):
        numer = numer + terms_ref[s]
        denom = denom + terms_ref[s + 1]
    corr = numer / (denom + 1.0)
    corr_ref[...] = corr
    stations = station_ref[...]
    high, low = stations >> 7, stations & (LANES - 1)
    found = jnp.zeros(stations.shape, F32)
    for h in range(corr.shape[0]):
        line = jnp.broadcast_to(corr[h : h + 1], stations.shape)
        found = jnp.where(high == h, jnp.take_along_axis(line, low, axis=1), found)
    weighted = weight_ref[...] * (misfit_ref[...] - found)
    weighted_ref[...] = weighted
    halves = weighted.astype(BF16).astype(F32)
    lane = iota(halves.shape, 1)
    left = lane < PICK_BLK
    turned = pltpu.roll(halves, PICK_BLK, 1)
    none = jnp.zeros_like(halves)
    tables = []
    for both in (jnp.where(left, halves, turned), jnp.where(left, turned, halves)):
        first, second = jnp.where(left, both, 0.0), jnp.where(left, 0.0, both)
        lower = jnp.concatenate([first, none, second, none], axis=0)
        upper = jnp.concatenate([none, first, none, second], axis=0)
        tables.append(jnp.concatenate([lower, upper], axis=1))
    table = jnp.concatenate(tables, axis=0).astype(BF16)
    matches = jnp.concatenate(row_matches(partials_ref), axis=1)
    sent = jnp.dot(matches, table, preferred_element_type=F32)
    peers = out_ref.shape[0]
    sent = [sent[:, t : t + LANES].reshape(peers, 8, LANES) for t in (0, LANES)]
    out_ref[...] = jnp.concatenate(sent, axis=1).astype(BF16)


def backward_kernel(code_ref, cell_ref, resid_ref, blocks_ref, corr_ref, weighted_ref,
                    out_ref, corr_hbm, weighted_hbm, terms_ref, sems):
    copies = [
        pltpu.make_async_copy(corr_ref, corr_hbm, sems.at[0]),
        pltpu.make_async_copy(weighted_ref, weighted_hbm, sems.at[1]),
    ]
    for copy in copies:
        copy.start()
    slots = blocks_ref.shape[0]
    lane, sub = iota((CHUNK, LANES), 1), iota((CHUNK, LANES), 0)
    sub_p = iota((2 * GROUP, LANES), 0) & (GROUP - 1)
    parity = sub & 1
    half = (lane >= PICK_BLK).astype(jnp.int32)
    for n in range(slots // CHUNK):
        code_down = down(code_ref[n : n + 1, :])
        row_of = code_down >> 1
        chosen = jnp.concatenate(
            [pick(row_of == lane + t) for t in range(0, resid_ref.shape[0], LANES)], axis=1
        )
        resid = jnp.dot(chosen, resid_ref[...], preferred_element_type=F32)
        resid = jnp.where((code_down & 1) == parity, resid, pltpu.roll(resid, PICK_BLK, 1))
        resid = jnp.where(half == parity, resid, 0.0)
        parts = []
        for j in range(0, CHUNK, 2 * GROUP):
            first = n * CHUNK + j
            both = [
                blocks_ref[k : k + GROUP].reshape(GROUP * PICK_BLK, CELL_BLK)
                for k in (first, first + GROUP)
            ]
            mine = resid[j : j + 2 * GROUP]
            wide = jnp.concatenate(
                [jnp.where((sub_p >> 1) == i, mine, 0.0) for i in range(GROUP // 2)], axis=1
            ).astype(BF16)
            terms = jnp.dot(wide, jnp.concatenate(both, axis=1), preferred_element_type=F32)
            parts += [terms[:GROUP, :LANES], terms[GROUP:, LANES:]]
        high, low = two_parts(jnp.concatenate(parts, axis=0))
        terms_ref[n * CHUNK : (n + 1) * CHUNK, 0:LANES] = high
        terms_ref[n * CHUNK : (n + 1) * CHUNK, LANES : 2 * LANES] = low
    cells_of = cell_ref[...]
    both = terms_ref[...]
    tile = 2 * LANES
    for t in range(0, out_ref.shape[1], tile):
        hot = jnp.concatenate(
            [pick(iota((tile, LANES), 0) + t == cells_of[r : r + 1]) for r in range(slots // LANES)],
            axis=1,
        )
        sums = jnp.dot(hot, both, preferred_element_type=F32)
        sums = (sums[:, :LANES] + sums[:, LANES:]).astype(BF16)
        for s in range(out_ref.shape[0]):
            out_ref[s, t : t + tile, :] = sums
    for copy in copies:
        copy.wait()


def gradient_kernel(terms_ref, out_hbm, total_ref, sems):
    pieces = sems.shape[0]
    rows = total_ref.shape[0] // pieces
    copies = []
    for n in range(pieces):
        at = pl.ds(n * rows, rows)
        total = terms_ref[0, at, :].astype(F32)
        for s in range(1, terms_ref.shape[0]):
            total = total + terms_ref[s, at, :].astype(F32)
        total_ref[at, :] = total
        copies.append(pltpu.make_async_copy(total_ref.at[at], out_hbm.at[at], sems.at[n]))
        copies[-1].start()
    for copy in copies:
        copy.wait()


def simple(kernel, out_shape, name, **more):
    return pl.pallas_call(
        kernel,
        out_shape=out_shape,
        compiler_params=pltpu.CompilerParams(vmem_limit_bytes=VMEM_BYTES),
        name=name,
        **more,
    )


def swap(x, axis, groups=None):
    return lax.all_to_all(x, axis, 0, 0, tiled=True, axis_index_groups=groups)


def torus_groups():
    lines, planes = {}, {}
    for x, zl, y, zh, c in itertools.product(range(4), range(2), range(4), range(4), range(2)):
        flat = (x * 2 + zl) * 32 + y * 8 + zh * 2 + c
        lines.setdefault((x, y), []).append(flat)
        planes.setdefault((zl, zh), []).append(flat)
    return list(lines.values()), list(planes.values())


def forward_call(count, picks_of, cells_of, model_rows, sensitivity, shells):
    slots = sensitivity.shape[0]
    return pl.pallas_call(
        forward_kernel,
        in_specs=[OUTSIDE] * 5,
        out_specs=(INSIDE,) * 3,
        out_shape=(
            jax.ShapeDtypeStruct((shells, SLOT_CAP + 8, LANES), BF16),
            jax.ShapeDtypeStruct(sensitivity.shape, BF16),
            jax.ShapeDtypeStruct(picks_of.shape, jnp.int32),
        ),
        scratch_shapes=[
            pltpu.SMEM((1,), jnp.int32),
            pltpu.VMEM(picks_of.shape, jnp.int32),
            pltpu.VMEM(cells_of.shape, jnp.int32),
            pltpu.VMEM(model_rows.shape, BF16),
            pltpu.VMEM((slots, 2 * LANES), BF16),
            pltpu.VMEM((shells * SLOT_CAP // 2, slots), BF16),
            pltpu.SemaphoreType.DMA((4,)),
            pltpu.SemaphoreType.DMA,
        ],
        compiler_params=pltpu.CompilerParams(vmem_limit_bytes=VMEM_BYTES),
        name="forward",
    )(
        count,
        *[
            pltpu.with_memory_space_constraint(v, pltpu.HBM)
            for v in (picks_of, cells_of, model_rows, sensitivity)
        ],
    )


def local(model, sensitivity, pick_block, cell_block, blk_count, observed, pick_weight, station):
    shells, events = lax.axis_size("shells"), lax.axis_size("events")
    picks_of = pick_block.reshape(-1, LANES)
    cells_of = cell_block.reshape(-1, LANES)
    model_rows = model.reshape(-1, CELL_BLK)
    observed, weight = observed.reshape(-1, LANES), pick_weight.reshape(-1, LANES)
    station = station.reshape(-1, LANES)
    own_rows = observed.shape[0]
    stat_rows = STATIONS // LANES
    shape = jax.ShapeDtypeStruct

    lines, planes = torus_groups()
    devices = ("events", "shells")

    slots = sensitivity.shape[0]
    q = SLOT_CAP // 2
    partials, blocks, codes = forward_call(blk_count, picks_of, cells_of, model_rows, sensitivity, shells)
    partials = swap(partials, "shells")
    misfit, stats = simple(
        stations_kernel,
        (
            shape((own_rows, LANES), F32),
            shape((len(lines[0]), stat_rows, LANES), F32),
        ),
        "stations",
    )(partials, observed, weight, station)
    stats = swap(stats, devices, lines)
    stats = simple(spread_kernel, shape((len(planes[0]), stat_rows, LANES), F32), "spread")(stats)
    stats = swap(stats, devices, planes)
    correction, weighted, halves = simple(
        weighted_kernel,
        (
            shape((STATIONS // LANES, LANES), F32),
            shape((own_rows, LANES), F32),
            shape((shells, q, LANES), BF16),
        ),
        "weighted",
    )(stats, misfit, weight, station, partials)
    halves = swap(halves, "shells").reshape(shells * q, LANES)
    grads, correction, weighted = simple(
        backward_kernel,
        (
            shape((events,) + model_rows.shape, BF16),
            shape(correction.shape, F32),
            shape(weighted.shape, F32),
        ),
        "backward",
        out_specs=(INSIDE, OUTSIDE, OUTSIDE),
        scratch_shapes=[pltpu.VMEM((slots, 2 * LANES), BF16), pltpu.SemaphoreType.DMA((2,))],
    )(codes, cells_of, halves, blocks, correction, weighted)
    grads = swap(grads, "events")
    gradient = simple(
        gradient_kernel,
        shape(model_rows.shape, F32),
        "gradient",
        out_specs=OUTSIDE,
        scratch_shapes=[pltpu.VMEM(model_rows.shape, F32), pltpu.SemaphoreType.DMA((4,))],
    )(grads)
    return (gradient.reshape(-1), correction.reshape(-1), weighted.reshape(-1))


def solution(mesh):
    both = P(("events", "shells"))
    placed = (P("shells"), P(("events", "shells"), None, None)) + (both,) * 6
    return jax.shard_map(
        local,
        mesh=mesh,
        in_specs=placed,
        out_specs=(P("shells"), P(), both),
        check_vma=False,
    )
```

```python
import itertools

import jax
import jax.numpy as jnp
from jax import lax
from jax.experimental import pallas as pl
from jax.experimental.pallas import tpu as pltpu
from jax.sharding import PartitionSpec as P

PICK_BLK = 64
CELL_BLK = 128
STATIONS = 2048
LANES = 128
GROUP = 8
CHUNK = 128
F32 = jnp.float32
BF16 = jnp.bfloat16
NT = (((1,), (1,)), ((), ()))
TN = (((0,), (0,)), ((), ()))
SLOT_CAP = 32
VMEM_BYTES = 40 << 20
PIECES = 4
OUTSIDE = pl.BlockSpec(memory_space=pltpu.HBM)
INSIDE = pl.BlockSpec(memory_space=pltpu.VMEM)


def iota(shape, axis):
    return lax.broadcasted_iota(jnp.int32, shape, axis)


def down(row):
    tall = jnp.broadcast_to(row.astype(F32), (LANES, LANES))
    return jnp.transpose(tall).astype(jnp.int32)


def pick(mask):
    return jnp.where(mask, 1.0, 0.0).astype(BF16)


def two_parts(x):
    high = x.astype(BF16)
    return high, (x - high.astype(F32)).astype(BF16)


def three_parts(x):
    high, rest = x.astype(BF16), x
    rest = x - high.astype(F32)
    mid = rest.astype(BF16)
    return high, mid, (rest - mid.astype(F32)).astype(BF16)


def forward_kernel(count_hbm, pick_hbm, cell_hbm, model_hbm, blocks_hbm, out_ref, blocks_ref, code_ref,
                   count, pick_ref, cell_ref, model_ref, values_ref, hot_ref, table_sems, block_sems):
    slots, cells = blocks_ref.shape[0], model_ref.shape[0]
    owners = out_ref.shape[0]
    chunks = range(slots // CHUNK)
    tables = [
        pltpu.make_async_copy(src, dst, table_sems.at[n])
        for n, (src, dst) in enumerate(
            [(count_hbm, count), (pick_hbm, pick_ref), (cell_hbm, cell_ref), (model_hbm, model_ref)]
        )
    ]
    for copy in tables:
        copy.start()
    piece = slots // block_sems.shape[0]

    def block_copy(n):
        at = pl.ds(n * piece, piece)
        return pltpu.make_async_copy(blocks_hbm.at[at], blocks_ref.at[at], block_sems.at[n])

    def start_copy(n, carry):
        block_copy(n).start()
        return carry

    lax.fori_loop(0, slots // piece, start_copy, 0)
    for copy in tables:
        copy.wait()
    lane, sub = iota((CHUNK, LANES), 1), iota((CHUNK, LANES), 0)
    half = (lane >= PICK_BLK).astype(jnp.int32)

    before, every = pick(sub < lane), jnp.ones((CHUNK, LANES), BF16)
    seen = jnp.zeros((owners, LANES), F32)
    index = jnp.zeros((owners * 8, LANES), F32)
    codes, code_down, rows = [], [], []
    for n in chunks:
        picks = pick_ref[n : n + 1, :]
        used = n * CHUNK + iota((1, LANES), 1) < count[0]
        owner, inside = picks >> 6, picks & (PICK_BLK - 1)
        mine = jnp.logical_and(iota((owners, LANES), 0) == owner, used)
        ones = pick(mine)
        ahead = seen + jnp.dot(ones, before, preferred_element_type=F32)
        seen = seen + jnp.dot(ones, every, preferred_element_type=F32)
        rank = jnp.sum(jnp.where(mine, ahead, 0.0), axis=0, keepdims=True).astype(jnp.int32)
        code = jnp.where(used, owner * SLOT_CAP + rank, -1)
        codes.append(code)
        code_ref[n : n + 1, :] = code
        code_down.append(down(code))
        cell_down = down(cell_ref[n : n + 1, :])
        chosen = jnp.concatenate([pick(cell_down == lane + t) for t in range(0, cells, LANES)], axis=1)
        rows.append(jnp.dot(chosen, model_ref[...], preferred_element_type=F32))
        tile_row = jnp.where(used, owner * 8 + ((code >> 1) & 7), -1)
        block = (inside & 1) * 32 + (inside >> 1) + 1
        tagged = iota((owners * 8, LANES), 0) == tile_row
        tagged = jnp.where(tagged, block.astype(F32), 0.0).astype(BF16)
        quarter = (code_down[n] & 1) * 2 + ((code_down[n] >> 4) & 1)
        index = index + jnp.dot(tagged, pick(lane >> 5 == quarter), preferred_element_type=F32)
        hot_ref[:, n * CHUNK : (n + 1) * CHUNK] = pick(iota((hot_ref.shape[0], LANES), 0) == code >> 1)
    out_ref[:, SLOT_CAP:, :] = index.astype(BF16).reshape(owners, 8, LANES)

    lane_g, sub_g = iota((GROUP, LANES), 1), iota((GROUP, LANES), 0)
    for n in chunks:
        parts = []
        for j in range(0, CHUNK, GROUP):
            first = n * CHUNK + j
            if first % piece == 0:
                block_copy(first // piece).wait()
            block = blocks_ref[first : first + GROUP].reshape(GROUP * PICK_BLK, CELL_BLK)
            wide = lax.dot_general(
                rows[n][j : j + GROUP].astype(BF16), block, NT, preferred_element_type=F32
            )
            part = jnp.zeros((GROUP, LANES), F32)
            for i in range(GROUP // 2):
                own = sub_g == 2 * i + (lane_g >= PICK_BLK).astype(jnp.int32)
                part = jnp.where(own, wide[:, i * LANES : (i + 1) * LANES], part)
            parts.append(part)
        values = jnp.concatenate(parts, axis=0)
        values = values + pltpu.roll(values, PICK_BLK, 1)
        values = jnp.where((code_down[n] & 1) == half, values, 0.0)
        high, low = two_parts(values)
        values_ref[n * CHUNK : (n + 1) * CHUNK, 0:LANES] = high
        values_ref[n * CHUNK : (n + 1) * CHUNK, LANES : 2 * LANES] = low
    placed = jnp.dot(hot_ref[...], values_ref[...], preferred_element_type=F32).astype(BF16)
    q = SLOT_CAP // 2
    out_ref[:, 0:q, :] = placed[:, :LANES].reshape(owners, q, LANES)
    out_ref[:, q : 2 * q, :] = placed[:, LANES:].reshape(owners, q, LANES)


def row_matches(terms_ref):
    tile = terms_ref[:, SLOT_CAP:, :].astype(F32).reshape(-1, LANES)
    lane = (iota(tile.shape, 1) & 31).astype(F32)
    return pick(tile == lane + 1.0), pick(tile == lane + 33.0)


def stations_kernel(terms_ref, observed_ref, weight_ref, station_ref, misfit_ref, out_ref):
    rows = observed_ref.shape[0]
    q = SLOT_CAP // 2

    def part(first):
        return terms_ref[:, first : first + 8, :].astype(F32).reshape(-1, LANES).astype(BF16)

    lower, upper = [jnp.concatenate([part(t), part(q + t)], axis=1) for t in (0, 8)]
    sides = []
    for match in row_matches(terms_ref):
        low_sum = lax.dot_general(match, lower, TN, preferred_element_type=F32)
        top_sum = lax.dot_general(match, upper, TN, preferred_element_type=F32)
        low_sum = low_sum[:, :LANES] + low_sum[:, LANES:]
        top_sum = top_sum[:, :LANES] + top_sum[:, LANES:]
        sides.append((low_sum[0:32] + top_sum[32:64], low_sum[64:96] + top_sum[96:128]))
    (even_left, even_right), (odd_left, odd_right) = sides
    predicted = jnp.where(
        iota((rows, LANES), 1) < PICK_BLK,
        even_left + pltpu.roll(even_right, PICK_BLK, 1),
        odd_right + pltpu.roll(odd_left, PICK_BLK, 1),
    )
    misfit = observed_ref[...] - predicted
    misfit_ref[...] = misfit
    weight = weight_ref[...]
    stations = station_ref[...]
    high, low = stations >> 7, stations & (LANES - 1)
    hi_count = STATIONS // LANES
    pieces = [p.astype(F32) for p in three_parts(weight * misfit) + three_parts(weight)]
    total = jnp.zeros((len(pieces) * hi_count, LANES), F32)
    for r0 in range(0, rows, 8):
        left, right = [], []
        for r in range(r0, r0 + 8):
            own = iota((hi_count, LANES), 0) == high[r : r + 1]
            left.append(
                jnp.concatenate([jnp.where(own, p[r : r + 1], 0.0) for p in pieces], axis=0).astype(BF16)
            )
            right.append(pick(iota((LANES, LANES), 0) == low[r : r + 1]))
        total = total + lax.dot_general(
            jnp.concatenate(left, axis=1), jnp.concatenate(right, axis=1), NT, preferred_element_type=F32
        )
    h = hi_count
    numer = total[0:h] + total[h : 2 * h] + total[2 * h : 3 * h]
    denom = total[3 * h : 4 * h] + total[4 * h : 5 * h] + total[5 * h : 6 * h]
    for s in range(out_ref.shape[0]):
        out_ref[s] = denom if s % 2 else numer


def spread_kernel(terms_ref, out_ref):
    total = terms_ref[0]
    for s in range(1, terms_ref.shape[0]):
        total = total + terms_ref[s]
    for s in range(out_ref.shape[0]):
        out_ref[s] = total


def weighted_kernel(terms_ref, misfit_ref, weight_ref, station_ref, partials_ref, corr_ref, weighted_ref, out_ref):
    numer, denom = terms_ref[0], terms_ref[1]
    for s in range(2, terms_ref.shape[0], 2):
        numer = numer + terms_ref[s]
        denom = denom + terms_ref[s + 1]
    corr = numer / (denom + 1.0)
    corr_ref[...] = corr
    stations = station_ref[...]
    high, low = stations >> 7, stations & (LANES - 1)
    found = jnp.zeros(stations.shape, F32)
    for h in range(corr.shape[0]):
        line = jnp.broadcast_to(corr[h : h + 1], stations.shape)
        found = jnp.where(high == h, jnp.take_along_axis(line, low, axis=1), found)
    weighted = weight_ref[...] * (misfit_ref[...] - found)
    weighted_ref[...] = weighted
    halves = weighted.astype(BF16).astype(F32)
    lane = iota(halves.shape, 1)
    left = lane < PICK_BLK
    turned = pltpu.roll(halves, PICK_BLK, 1)
    none = jnp.zeros_like(halves)
    tables = []
    for both in (jnp.where(left, halves, turned), jnp.where(left, turned, halves)):
        first, second = jnp.where(left, both, 0.0), jnp.where(left, 0.0, both)
        lower = jnp.concatenate([first, none, second, none], axis=0)
        upper = jnp.concatenate([none, first, none, second], axis=0)
        tables.append(jnp.concatenate([lower, upper], axis=1))
    table = jnp.concatenate(tables, axis=0).astype(BF16)
    matches = jnp.concatenate(row_matches(partials_ref), axis=1)
    sent = jnp.dot(matches, table, preferred_element_type=F32)
    peers = out_ref.shape[0]
    sent = [sent[:, t : t + LANES].reshape(peers, 8, LANES) for t in (0, LANES)]
    out_ref[...] = jnp.concatenate(sent, axis=1).astype(BF16)


def backward_kernel(code_ref, cell_ref, resid_ref, blocks_ref, corr_ref, weighted_ref,
                    out_ref, corr_hbm, weighted_hbm, terms_ref, sems):
    copies = [
        pltpu.make_async_copy(corr_ref, corr_hbm, sems.at[0]),
        pltpu.make_async_copy(weighted_ref, weighted_hbm, sems.at[1]),
    ]
    for copy in copies:
        copy.start()
    slots = blocks_ref.shape[0]
    lane, sub = iota((CHUNK, LANES), 1), iota((CHUNK, LANES), 0)
    sub_p = iota((2 * GROUP, LANES), 0) & (GROUP - 1)
    parity = sub & 1
    half = (lane >= PICK_BLK).astype(jnp.int32)
    for n in range(slots // CHUNK):
        code_down = down(code_ref[n : n + 1, :])
        row_of = code_down >> 1
        chosen = jnp.concatenate(
            [pick(row_of == lane + t) for t in range(0, resid_ref.shape[0], LANES)], axis=1
        )
        resid = jnp.dot(chosen, resid_ref[...], preferred_element_type=F32)
        resid = jnp.where((code_down & 1) == parity, resid, pltpu.roll(resid, PICK_BLK, 1))
        resid = jnp.where(half == parity, resid, 0.0)
        parts = []
        for j in range(0, CHUNK, 2 * GROUP):
            first = n * CHUNK + j
            both = [
                blocks_ref[k : k + GROUP].reshape(GROUP * PICK_BLK, CELL_BLK)
                for k in (first, first + GROUP)
            ]
            mine = resid[j : j + 2 * GROUP]
            wide = jnp.concatenate(
                [jnp.where((sub_p >> 1) == i, mine, 0.0) for i in range(GROUP // 2)], axis=1
            ).astype(BF16)
            terms = jnp.dot(wide, jnp.concatenate(both, axis=1), preferred_element_type=F32)
            parts += [terms[:GROUP, :LANES], terms[GROUP:, LANES:]]
        high, low = two_parts(jnp.concatenate(parts, axis=0))
        terms_ref[n * CHUNK : (n + 1) * CHUNK, 0:LANES] = high
        terms_ref[n * CHUNK : (n + 1) * CHUNK, LANES : 2 * LANES] = low
    cells_of = cell_ref[...]
    both = terms_ref[...]
    tile = 2 * LANES
    for t in range(0, out_ref.shape[0], tile):
        hot = jnp.concatenate(
            [pick(iota((tile, LANES), 0) + t == cells_of[r : r + 1]) for r in range(slots // LANES)],
            axis=1,
        )
        sums = jnp.dot(hot, both, preferred_element_type=F32)
        sums = (sums[:, :LANES] + sums[:, LANES:]).astype(BF16)
        out_ref[t : t + tile, :] = sums
    for copy in copies:
        copy.wait()


def pair_kernel(own_ref, other_ref, out_ref):
    total = (own_ref[...].astype(F32) + other_ref[...].astype(F32)).astype(BF16)
    for s in range(out_ref.shape[0]):
        out_ref[s] = total


def gradient_kernel(terms_ref, out_hbm, total_ref, sems):
    pieces = sems.shape[0]
    rows = total_ref.shape[0] // pieces
    copies = []
    for n in range(pieces):
        at = pl.ds(n * rows, rows)
        total = terms_ref[0, at, :].astype(F32)
        for s in range(1, terms_ref.shape[0]):
            total = total + terms_ref[s, at, :].astype(F32)
        total_ref[at, :] = total
        copies.append(pltpu.make_async_copy(total_ref.at[at], out_hbm.at[at], sems.at[n]))
        copies[-1].start()
    for copy in copies:
        copy.wait()


def simple(kernel, out_shape, name, **more):
    return pl.pallas_call(
        kernel,
        out_shape=out_shape,
        compiler_params=pltpu.CompilerParams(vmem_limit_bytes=VMEM_BYTES),
        name=name,
        **more,
    )


def swap(x, axis, groups=None):
    return lax.all_to_all(x, axis, 0, 0, tiled=True, axis_index_groups=groups)


def torus_groups():
    lines, planes = {}, {}
    for x, zl, y, zh, c in itertools.product(range(4), range(2), range(4), range(4), range(2)):
        flat = (x * 2 + zl) * 32 + y * 8 + zh * 2 + c
        lines.setdefault((x, y), []).append(flat)
        planes.setdefault((zl, zh), []).append(flat)
    return list(lines.values()), list(planes.values())


def forward_call(count, picks_of, cells_of, model_rows, sensitivity, shells):
    slots = sensitivity.shape[0]
    return pl.pallas_call(
        forward_kernel,
        in_specs=[OUTSIDE] * 5,
        out_specs=(INSIDE,) * 3,
        out_shape=(
            jax.ShapeDtypeStruct((shells, SLOT_CAP + 8, LANES), BF16),
            jax.ShapeDtypeStruct(sensitivity.shape, BF16),
            jax.ShapeDtypeStruct(picks_of.shape, jnp.int32),
        ),
        scratch_shapes=[
            pltpu.SMEM((1,), jnp.int32),
            pltpu.VMEM(picks_of.shape, jnp.int32),
            pltpu.VMEM(cells_of.shape, jnp.int32),
            pltpu.VMEM(model_rows.shape, BF16),
            pltpu.VMEM((slots, 2 * LANES), BF16),
            pltpu.VMEM((shells * SLOT_CAP // 2, slots), BF16),
            pltpu.SemaphoreType.DMA((4,)),
            pltpu.SemaphoreType.DMA((PIECES,)),
        ],
        compiler_params=pltpu.CompilerParams(vmem_limit_bytes=VMEM_BYTES),
        name="forward",
    )(
        count,
        *[
            pltpu.with_memory_space_constraint(v, pltpu.HBM)
            for v in (picks_of, cells_of, model_rows, sensitivity)
        ],
    )


def local(model, sensitivity, pick_block, cell_block, blk_count, observed, pick_weight, station):
    shells, events = lax.axis_size("shells"), lax.axis_size("events")
    picks_of = pick_block.reshape(-1, LANES)
    cells_of = cell_block.reshape(-1, LANES)
    model_rows = model.reshape(-1, CELL_BLK)
    observed, weight = observed.reshape(-1, LANES), pick_weight.reshape(-1, LANES)
    station = station.reshape(-1, LANES)
    own_rows = observed.shape[0]
    stat_rows = STATIONS // LANES
    shape = jax.ShapeDtypeStruct

    lines, planes = torus_groups()
    devices = ("events", "shells")

    slots = sensitivity.shape[0]
    q = SLOT_CAP // 2
    partials, blocks, codes = forward_call(blk_count, picks_of, cells_of, model_rows, sensitivity, shells)
    partials = swap(partials, "shells")
    misfit, stats = simple(
        stations_kernel,
        (
            shape((own_rows, LANES), F32),
            shape((len(lines[0]), stat_rows, LANES), F32),
        ),
        "stations",
    )(partials, observed, weight, station)
    stats = swap(stats, devices, lines)
    stats = simple(spread_kernel, shape((len(planes[0]), stat_rows, LANES), F32), "spread")(stats)
    stats = swap(stats, devices, planes)
    correction, weighted, halves = simple(
        weighted_kernel,
        (
            shape((STATIONS // LANES, LANES), F32),
            shape((own_rows, LANES), F32),
            shape((shells, q, LANES), BF16),
        ),
        "weighted",
    )(stats, misfit, weight, station, partials)
    halves = swap(halves, "shells").reshape(shells * q, LANES)
    grads, correction, weighted = simple(
        backward_kernel,
        (
            shape(model_rows.shape, BF16),
            shape(correction.shape, F32),
            shape(weighted.shape, F32),
        ),
        "backward",
        out_specs=(INSIDE, OUTSIDE, OUTSIDE),
        scratch_shapes=[pltpu.VMEM((slots, 2 * LANES), BF16), pltpu.SemaphoreType.DMA((2,))],
    )(codes, cells_of, halves, blocks, correction, weighted)
    other = lax.ppermute(grads, "events", [(e, e ^ 1) for e in range(events)])
    grads = simple(pair_kernel, shape((events // 2,) + model_rows.shape, BF16), "pair")(grads, other)
    grads = swap(grads, "events", [list(range(e, events, 2)) for e in (0, 1)])
    gradient = simple(
        gradient_kernel,
        shape(model_rows.shape, F32),
        "gradient",
        out_specs=OUTSIDE,
        scratch_shapes=[pltpu.VMEM(model_rows.shape, F32), pltpu.SemaphoreType.DMA((4,))],
    )(grads)
    return (gradient.reshape(-1), correction.reshape(-1), weighted.reshape(-1))


def solution(mesh):
    both = P(("events", "shells"))
    placed = (P("shells"), P(("events", "shells"), None, None)) + (both,) * 6
    return jax.shard_map(
        local,
        mesh=mesh,
        in_specs=placed,
        out_specs=(P("shells"), P(), both),
        check_vma=False,
    )
```

```python
import itertools

import jax
import jax.numpy as jnp
from jax import lax
from jax.experimental import pallas as pl
from jax.experimental.pallas import tpu as pltpu
from jax.sharding import PartitionSpec as P

PICK_BLK = 64
CELL_BLK = 128
STATIONS = 2048
LANES = 128
GROUP = 8
CHUNK = 128
F32 = jnp.float32
BF16 = jnp.bfloat16
NT = (((1,), (1,)), ((), ()))
TN = (((0,), (0,)), ((), ()))
SLOT_CAP = 32
VMEM_BYTES = 40 << 20
PIECES = 4
OUTSIDE = pl.BlockSpec(memory_space=pltpu.HBM)
INSIDE = pl.BlockSpec(memory_space=pltpu.VMEM)


def iota(shape, axis):
    return lax.broadcasted_iota(jnp.int32, shape, axis)


def down(row):
    tall = jnp.broadcast_to(row.astype(F32), (LANES, LANES))
    return jnp.transpose(tall).astype(jnp.int32)


def pick(mask):
    return jnp.where(mask, 1.0, 0.0).astype(BF16)


def two_parts(x):
    high = x.astype(BF16)
    return high, (x - high.astype(F32)).astype(BF16)


def three_parts(x):
    high, rest = x.astype(BF16), x
    rest = x - high.astype(F32)
    mid = rest.astype(BF16)
    return high, mid, (rest - mid.astype(F32)).astype(BF16)


def forward_kernel(count_hbm, pick_hbm, cell_hbm, model_hbm, blocks_hbm, out_ref, blocks_ref, code_ref,
                   count, pick_ref, cell_ref, model_ref, values_ref, hot_ref, table_sems, block_sems):
    slots, cells = blocks_ref.shape[0], model_ref.shape[0]
    owners = out_ref.shape[0]
    chunks = range(slots // CHUNK)
    tables = [
        pltpu.make_async_copy(src, dst, table_sems.at[n])
        for n, (src, dst) in enumerate(
            [(count_hbm, count), (pick_hbm, pick_ref), (cell_hbm, cell_ref), (model_hbm, model_ref)]
        )
    ]
    for copy in tables:
        copy.start()
    piece = slots // block_sems.shape[0]

    def block_copy(n):
        at = pl.ds(n * piece, piece)
        return pltpu.make_async_copy(blocks_hbm.at[at], blocks_ref.at[at], block_sems.at[n])

    def start_copy(n, carry):
        block_copy(n).start()
        return carry

    lax.fori_loop(0, slots // piece, start_copy, 0)
    for copy in tables:
        copy.wait()
    lane, sub = iota((CHUNK, LANES), 1), iota((CHUNK, LANES), 0)
    half = (lane >= PICK_BLK).astype(jnp.int32)

    before, every = pick(sub < lane), jnp.ones((CHUNK, LANES), BF16)
    seen = jnp.zeros((owners, LANES), F32)
    index = jnp.zeros((owners * 8, LANES), F32)
    codes, code_down, rows = [], [], []
    for n in chunks:
        picks = pick_ref[n : n + 1, :]
        used = n * CHUNK + iota((1, LANES), 1) < count[0]
        owner, inside = picks >> 6, picks & (PICK_BLK - 1)
        mine = jnp.logical_and(iota((owners, LANES), 0) == owner, used)
        ones = pick(mine)
        ahead = seen + jnp.dot(ones, before, preferred_element_type=F32)
        seen = seen + jnp.dot(ones, every, preferred_element_type=F32)
        rank = jnp.sum(jnp.where(mine, ahead, 0.0), axis=0, keepdims=True).astype(jnp.int32)
        code = jnp.where(used, owner * SLOT_CAP + rank, -1)
        codes.append(code)
        code_ref[n : n + 1, :] = code
        code_down.append(down(code))
        cell_down = down(cell_ref[n : n + 1, :])
        chosen = jnp.concatenate([pick(cell_down == lane + t) for t in range(0, cells, LANES)], axis=1)
        rows.append(jnp.dot(chosen, model_ref[...], preferred_element_type=F32))
        tile_row = jnp.where(used, owner * 8 + ((code >> 1) & 7), -1)
        block = (inside & 1) * 32 + (inside >> 1) + 1
        tagged = iota((owners * 8, LANES), 0) == tile_row
        tagged = jnp.where(tagged, block.astype(F32), 0.0).astype(BF16)
        quarter = (code_down[n] & 1) * 2 + ((code_down[n] >> 4) & 1)
        index = index + jnp.dot(tagged, pick(lane >> 5 == quarter), preferred_element_type=F32)
        hot_ref[:, n * CHUNK : (n + 1) * CHUNK] = pick(iota((hot_ref.shape[0], LANES), 0) == code >> 1)
    out_ref[:, SLOT_CAP:, :] = index.astype(BF16).reshape(owners, 8, LANES)

    lane_g, sub_g = iota((GROUP, LANES), 1), iota((GROUP, LANES), 0)
    for n in chunks:
        parts = []
        for j in range(0, CHUNK, GROUP):
            first = n * CHUNK + j
            if first % piece == 0:
                block_copy(first // piece).wait()
            block = blocks_ref[first : first + GROUP].reshape(GROUP * PICK_BLK, CELL_BLK)
            wide = lax.dot_general(
                rows[n][j : j + GROUP].astype(BF16), block, NT, preferred_element_type=F32
            )
            part = jnp.zeros((GROUP, LANES), F32)
            for i in range(GROUP // 2):
                own = sub_g == 2 * i + (lane_g >= PICK_BLK).astype(jnp.int32)
                part = jnp.where(own, wide[:, i * LANES : (i + 1) * LANES], part)
            parts.append(part)
        values = jnp.concatenate(parts, axis=0)
        values = values + pltpu.roll(values, PICK_BLK, 1)
        values = jnp.where((code_down[n] & 1) == half, values, 0.0)
        high, low = two_parts(values)
        values_ref[n * CHUNK : (n + 1) * CHUNK, 0:LANES] = high
        values_ref[n * CHUNK : (n + 1) * CHUNK, LANES : 2 * LANES] = low
    placed = jnp.dot(hot_ref[...], values_ref[...], preferred_element_type=F32).astype(BF16)
    q = SLOT_CAP // 2
    out_ref[:, 0:q, :] = placed[:, :LANES].reshape(owners, q, LANES)
    out_ref[:, q : 2 * q, :] = placed[:, LANES:].reshape(owners, q, LANES)


def row_matches(terms_ref):
    tile = terms_ref[:, SLOT_CAP:, :].astype(F32).reshape(-1, LANES)
    lane = (iota(tile.shape, 1) & 31).astype(F32)
    return pick(tile == lane + 1.0), pick(tile == lane + 33.0)


def stations_kernel(terms_ref, observed_ref, weight_ref, station_ref, misfit_ref, out_ref):
    rows = observed_ref.shape[0]
    q = SLOT_CAP // 2

    def part(first):
        return terms_ref[:, first : first + 8, :].astype(F32).reshape(-1, LANES).astype(BF16)

    lower, upper = [jnp.concatenate([part(t), part(q + t)], axis=1) for t in (0, 8)]
    sides = []
    for match in row_matches(terms_ref):
        low_sum = lax.dot_general(match, lower, TN, preferred_element_type=F32)
        top_sum = lax.dot_general(match, upper, TN, preferred_element_type=F32)
        low_sum = low_sum[:, :LANES] + low_sum[:, LANES:]
        top_sum = top_sum[:, :LANES] + top_sum[:, LANES:]
        sides.append((low_sum[0:32] + top_sum[32:64], low_sum[64:96] + top_sum[96:128]))
    (even_left, even_right), (odd_left, odd_right) = sides
    predicted = jnp.where(
        iota((rows, LANES), 1) < PICK_BLK,
        even_left + pltpu.roll(even_right, PICK_BLK, 1),
        odd_right + pltpu.roll(odd_left, PICK_BLK, 1),
    )
    misfit = observed_ref[...] - predicted
    misfit_ref[...] = misfit
    weight = weight_ref[...]
    stations = station_ref[...]
    high, low = stations >> 7, stations & (LANES - 1)
    hi_count = STATIONS // LANES
    pieces = [p.astype(F32) for p in three_parts(weight * misfit) + three_parts(weight)]
    total = jnp.zeros((len(pieces) * hi_count, LANES), F32)
    for r0 in range(0, rows, 8):
        left, right = [], []
        for r in range(r0, r0 + 8):
            own = iota((hi_count, LANES), 0) == high[r : r + 1]
            left.append(
                jnp.concatenate([jnp.where(own, p[r : r + 1], 0.0) for p in pieces], axis=0).astype(BF16)
            )
            right.append(pick(iota((LANES, LANES), 0) == low[r : r + 1]))
        total = total + lax.dot_general(
            jnp.concatenate(left, axis=1), jnp.concatenate(right, axis=1), NT, preferred_element_type=F32
        )
    h = hi_count
    numer = total[0:h] + total[h : 2 * h] + total[2 * h : 3 * h]
    denom = total[3 * h : 4 * h] + total[4 * h : 5 * h] + total[5 * h : 6 * h]
    for s in range(out_ref.shape[0]):
        out_ref[s] = denom if s % 2 else numer


def spread_kernel(terms_ref, out_ref):
    total = terms_ref[0]
    for s in range(1, terms_ref.shape[0]):
        total = total + terms_ref[s]
    for s in range(out_ref.shape[0]):
        out_ref[s] = total


def weighted_kernel(terms_ref, misfit_ref, weight_ref, station_ref, partials_ref, corr_ref, weighted_ref, out_ref):
    numer, denom = terms_ref[0], terms_ref[1]
    for s in range(2, terms_ref.shape[0], 2):
        numer = numer + terms_ref[s]
        denom = denom + terms_ref[s + 1]
    corr = numer / (denom + 1.0)
    corr_ref[...] = corr
    stations = station_ref[...]
    high, low = stations >> 7, stations & (LANES - 1)
    found = jnp.zeros(stations.shape, F32)
    for h in range(corr.shape[0]):
        line = jnp.broadcast_to(corr[h : h + 1], stations.shape)
        found = jnp.where(high == h, jnp.take_along_axis(line, low, axis=1), found)
    weighted = weight_ref[...] * (misfit_ref[...] - found)
    weighted_ref[...] = weighted
    halves = weighted.astype(BF16).astype(F32)
    lane = iota(halves.shape, 1)
    left = lane < PICK_BLK
    turned = pltpu.roll(halves, PICK_BLK, 1)
    none = jnp.zeros_like(halves)
    tables = []
    for both in (jnp.where(left, halves, turned), jnp.where(left, turned, halves)):
        first, second = jnp.where(left, both, 0.0), jnp.where(left, 0.0, both)
        lower = jnp.concatenate([first, none, second, none], axis=0)
        upper = jnp.concatenate([none, first, none, second], axis=0)
        tables.append(jnp.concatenate([lower, upper], axis=1))
    table = jnp.concatenate(tables, axis=0).astype(BF16)
    matches = jnp.concatenate(row_matches(partials_ref), axis=1)
    sent = jnp.dot(matches, table, preferred_element_type=F32)
    peers = out_ref.shape[0]
    sent = [sent[:, t : t + LANES].reshape(peers, 8, LANES) for t in (0, LANES)]
    out_ref[...] = jnp.concatenate(sent, axis=1).astype(BF16)


def backward_kernel(code_ref, cell_ref, resid_ref, blocks_ref, corr_ref, weighted_ref,
                    keep_ref, send_ref, corr_hbm, weighted_hbm, terms_ref, sems):
    copies = [
        pltpu.make_async_copy(corr_ref, corr_hbm, sems.at[0]),
        pltpu.make_async_copy(weighted_ref, weighted_hbm, sems.at[1]),
    ]
    for copy in copies:
        copy.start()
    slots = blocks_ref.shape[0]
    lane, sub = iota((CHUNK, LANES), 1), iota((CHUNK, LANES), 0)
    sub_p = iota((2 * GROUP, LANES), 0) & (GROUP - 1)
    parity = sub & 1
    half = (lane >= PICK_BLK).astype(jnp.int32)
    for n in range(slots // CHUNK):
        code_down = down(code_ref[n : n + 1, :])
        row_of = code_down >> 1
        chosen = jnp.concatenate(
            [pick(row_of == lane + t) for t in range(0, resid_ref.shape[0], LANES)], axis=1
        )
        resid = jnp.dot(chosen, resid_ref[...], preferred_element_type=F32)
        resid = jnp.where((code_down & 1) == parity, resid, pltpu.roll(resid, PICK_BLK, 1))
        resid = jnp.where(half == parity, resid, 0.0)
        parts = []
        for j in range(0, CHUNK, 2 * GROUP):
            first = n * CHUNK + j
            both = [
                blocks_ref[k : k + GROUP].reshape(GROUP * PICK_BLK, CELL_BLK)
                for k in (first, first + GROUP)
            ]
            mine = resid[j : j + 2 * GROUP]
            wide = jnp.concatenate(
                [jnp.where((sub_p >> 1) == i, mine, 0.0) for i in range(GROUP // 2)], axis=1
            ).astype(BF16)
            terms = jnp.dot(wide, jnp.concatenate(both, axis=1), preferred_element_type=F32)
            parts += [terms[:GROUP, :LANES], terms[GROUP:, LANES:]]
        high, low = two_parts(jnp.concatenate(parts, axis=0))
        terms_ref[n * CHUNK : (n + 1) * CHUNK, 0:LANES] = high
        terms_ref[n * CHUNK : (n + 1) * CHUNK, LANES : 2 * LANES] = low
    cells_of = cell_ref[...]
    both = terms_ref[...]
    cells = keep_ref.shape[0]
    parity = lax.axis_index("events") & 1
    for ref, side in ((send_ref, 1 - parity), (keep_ref, parity)):
        inside = cells_of - side * cells
        hot = jnp.concatenate(
            [pick(iota((cells, LANES), 0) == inside[r : r + 1]) for r in range(slots // LANES)], axis=1
        )
        sums = jnp.dot(hot, both, preferred_element_type=F32)
        ref[...] = (sums[:, :LANES] + sums[:, LANES:]).astype(ref.dtype)
    for copy in copies:
        copy.wait()


def pair_kernel(own_ref, other_ref, out_ref):
    total = (own_ref[...] + other_ref[...].astype(F32)).astype(BF16)
    for s in range(out_ref.shape[0]):
        out_ref[s] = total


def gradient_kernel(terms_ref, out_hbm, total_ref, sems):
    pieces = sems.shape[0]
    rows = total_ref.shape[0] // pieces
    copies = []
    for n in range(pieces):
        side, start = divmod(n * rows, terms_ref.shape[1])
        total = terms_ref[side, start : start + rows, :].astype(F32)
        for s in range(side + 2, terms_ref.shape[0], 2):
            total = total + terms_ref[s, start : start + rows, :].astype(F32)
        at = pl.ds(n * rows, rows)
        total_ref[at, :] = total
        copies.append(pltpu.make_async_copy(total_ref.at[at], out_hbm.at[at], sems.at[n]))
        copies[-1].start()
    for copy in copies:
        copy.wait()


def simple(kernel, out_shape, name, **more):
    return pl.pallas_call(
        kernel,
        out_shape=out_shape,
        compiler_params=pltpu.CompilerParams(vmem_limit_bytes=VMEM_BYTES),
        name=name,
        **more,
    )


def swap(x, axis, groups=None):
    return lax.all_to_all(x, axis, 0, 0, tiled=True, axis_index_groups=groups)


def torus_groups():
    lines, planes = {}, {}
    for x, zl, y, zh, c in itertools.product(range(4), range(2), range(4), range(4), range(2)):
        flat = (x * 2 + zl) * 32 + y * 8 + zh * 2 + c
        lines.setdefault((x, y), []).append(flat)
        planes.setdefault((zl, zh), []).append(flat)
    return list(lines.values()), list(planes.values())


def forward_call(count, picks_of, cells_of, model_rows, sensitivity, shells):
    slots = sensitivity.shape[0]
    return pl.pallas_call(
        forward_kernel,
        in_specs=[OUTSIDE] * 5,
        out_specs=(INSIDE,) * 3,
        out_shape=(
            jax.ShapeDtypeStruct((shells, SLOT_CAP + 8, LANES), BF16),
            jax.ShapeDtypeStruct(sensitivity.shape, BF16),
            jax.ShapeDtypeStruct(picks_of.shape, jnp.int32),
        ),
        scratch_shapes=[
            pltpu.SMEM((1,), jnp.int32),
            pltpu.VMEM(picks_of.shape, jnp.int32),
            pltpu.VMEM(cells_of.shape, jnp.int32),
            pltpu.VMEM(model_rows.shape, BF16),
            pltpu.VMEM((slots, 2 * LANES), BF16),
            pltpu.VMEM((shells * SLOT_CAP // 2, slots), BF16),
            pltpu.SemaphoreType.DMA((4,)),
            pltpu.SemaphoreType.DMA((PIECES,)),
        ],
        compiler_params=pltpu.CompilerParams(vmem_limit_bytes=VMEM_BYTES),
        name="forward",
    )(
        count,
        *[
            pltpu.with_memory_space_constraint(v, pltpu.HBM)
            for v in (picks_of, cells_of, model_rows, sensitivity)
        ],
    )


def local(model, sensitivity, pick_block, cell_block, blk_count, observed, pick_weight, station):
    shells, events = lax.axis_size("shells"), lax.axis_size("events")
    picks_of = pick_block.reshape(-1, LANES)
    cells_of = cell_block.reshape(-1, LANES)
    model_rows = model.reshape(-1, CELL_BLK)
    observed, weight = observed.reshape(-1, LANES), pick_weight.reshape(-1, LANES)
    station = station.reshape(-1, LANES)
    own_rows = observed.shape[0]
    stat_rows = STATIONS // LANES
    shape = jax.ShapeDtypeStruct

    lines, planes = torus_groups()
    devices = ("events", "shells")

    slots = sensitivity.shape[0]
    q = SLOT_CAP // 2
    partials, blocks, codes = forward_call(blk_count, picks_of, cells_of, model_rows, sensitivity, shells)
    partials = swap(partials, "shells")
    misfit, stats = simple(
        stations_kernel,
        (
            shape((own_rows, LANES), F32),
            shape((len(lines[0]), stat_rows, LANES), F32),
        ),
        "stations",
    )(partials, observed, weight, station)
    stats = swap(stats, devices, lines)
    stats = simple(spread_kernel, shape((len(planes[0]), stat_rows, LANES), F32), "spread")(stats)
    stats = swap(stats, devices, planes)
    correction, weighted, halves = simple(
        weighted_kernel,
        (
            shape((STATIONS // LANES, LANES), F32),
            shape((own_rows, LANES), F32),
            shape((shells, q, LANES), BF16),
        ),
        "weighted",
    )(stats, misfit, weight, station, partials)
    halves = swap(halves, "shells").reshape(shells * q, LANES)
    half_cells = (model_rows.shape[0] // 2, LANES)
    kept, sent, correction, weighted = simple(
        backward_kernel,
        (
            shape(half_cells, F32),
            shape(half_cells, BF16),
            shape(correction.shape, F32),
            shape(weighted.shape, F32),
        ),
        "backward",
        out_specs=(INSIDE, INSIDE, OUTSIDE, OUTSIDE),
        scratch_shapes=[pltpu.VMEM((slots, 2 * LANES), BF16), pltpu.SemaphoreType.DMA((2,))],
    )(codes, cells_of, halves, blocks, correction, weighted)
    other = lax.ppermute(sent, "events", [(e, e ^ 1) for e in range(events)])
    grads = simple(pair_kernel, shape((events,) + half_cells, BF16), "pair")(kept, other)
    grads = swap(grads, "events")
    gradient = simple(
        gradient_kernel,
        shape(model_rows.shape, F32),
        "gradient",
        out_specs=OUTSIDE,
        scratch_shapes=[pltpu.VMEM(model_rows.shape, F32), pltpu.SemaphoreType.DMA((4,))],
    )(grads)
    return (gradient.reshape(-1), correction.reshape(-1), weighted.reshape(-1))


def solution(mesh):
    both = P(("events", "shells"))
    placed = (P("shells"), P(("events", "shells"), None, None)) + (both,) * 6
    return jax.shard_map(
        local,
        mesh=mesh,
        in_specs=placed,
        out_specs=(P("shells"), P(), both),
        check_vma=False,
    )
```

```python
import itertools

import jax
import jax.numpy as jnp
from jax import lax
from jax.experimental import pallas as pl
from jax.experimental.pallas import tpu as pltpu
from jax.sharding import PartitionSpec as P

PICK_BLK = 64
CELL_BLK = 128
STATIONS = 2048
LANES = 128
GROUP = 8
CHUNK = 128
F32 = jnp.float32
BF16 = jnp.bfloat16
NT = (((1,), (1,)), ((), ()))
TN = (((0,), (0,)), ((), ()))
SLOT_CAP = 32
VMEM_BYTES = 40 << 20
PIECES = 4
OUTSIDE = pl.BlockSpec(memory_space=pltpu.HBM)
INSIDE = pl.BlockSpec(memory_space=pltpu.VMEM)


def iota(shape, axis):
    return lax.broadcasted_iota(jnp.int32, shape, axis)


def down(row):
    tall = jnp.broadcast_to(row.astype(F32), (LANES, LANES))
    return jnp.transpose(tall).astype(jnp.int32)


def pick(mask):
    return jnp.where(mask, 1.0, 0.0).astype(BF16)


def two_parts(x):
    high = x.astype(BF16)
    return high, (x - high.astype(F32)).astype(BF16)


def three_parts(x):
    high, rest = x.astype(BF16), x
    rest = x - high.astype(F32)
    mid = rest.astype(BF16)
    return high, mid, (rest - mid.astype(F32)).astype(BF16)


def forward_kernel(count_hbm, pick_hbm, cell_hbm, model_hbm, blocks_hbm, out_ref, blocks_ref, code_ref, side_ref,
                   count, pick_ref, cell_ref, model_ref, values_ref, hot_ref, table_sems, block_sems):
    slots, cells = blocks_ref.shape[0], model_ref.shape[0]
    owners = out_ref.shape[0]
    chunks = range(slots // CHUNK)
    tables = [
        pltpu.make_async_copy(src, dst, table_sems.at[n])
        for n, (src, dst) in enumerate(
            [(count_hbm, count), (pick_hbm, pick_ref), (cell_hbm, cell_ref), (model_hbm, model_ref)]
        )
    ]
    for copy in tables:
        copy.start()
    piece = slots // block_sems.shape[0]

    def block_copy(n):
        at = pl.ds(n * piece, piece)
        return pltpu.make_async_copy(blocks_hbm.at[at], blocks_ref.at[at], block_sems.at[n])

    def start_copy(n, carry):
        block_copy(n).start()
        return carry

    lax.fori_loop(0, slots // piece, start_copy, 0)
    for copy in tables:
        copy.wait()
    lane, sub = iota((CHUNK, LANES), 1), iota((CHUNK, LANES), 0)
    half = (lane >= PICK_BLK).astype(jnp.int32)
    side_ref[...] = cell_ref[...] - (lax.axis_index("events") & 1) * (cells // 2)

    before, every = pick(sub < lane), jnp.ones((CHUNK, LANES), BF16)
    seen = jnp.zeros((owners, LANES), F32)
    index = jnp.zeros((owners * 8, LANES), F32)
    codes, code_down, rows = [], [], []
    for n in chunks:
        picks = pick_ref[n : n + 1, :]
        used = n * CHUNK + iota((1, LANES), 1) < count[0]
        owner, inside = picks >> 6, picks & (PICK_BLK - 1)
        mine = jnp.logical_and(iota((owners, LANES), 0) == owner, used)
        ones = pick(mine)
        ahead = seen + jnp.dot(ones, before, preferred_element_type=F32)
        seen = seen + jnp.dot(ones, every, preferred_element_type=F32)
        rank = jnp.sum(jnp.where(mine, ahead, 0.0), axis=0, keepdims=True).astype(jnp.int32)
        code = jnp.where(used, owner * SLOT_CAP + rank, -1)
        codes.append(code)
        code_ref[n : n + 1, :] = code
        code_down.append(down(code))
        cell_down = down(cell_ref[n : n + 1, :])
        chosen = jnp.concatenate([pick(cell_down == lane + t) for t in range(0, cells, LANES)], axis=1)
        rows.append(jnp.dot(chosen, model_ref[...], preferred_element_type=F32))
        tile_row = jnp.where(used, owner * 8 + ((code >> 1) & 7), -1)
        block = (inside & 1) * 32 + (inside >> 1) + 1
        tagged = iota((owners * 8, LANES), 0) == tile_row
        tagged = jnp.where(tagged, block.astype(F32), 0.0).astype(BF16)
        quarter = (code_down[n] & 1) * 2 + ((code_down[n] >> 4) & 1)
        index = index + jnp.dot(tagged, pick(lane >> 5 == quarter), preferred_element_type=F32)
        hot_ref[:, n * CHUNK : (n + 1) * CHUNK] = pick(iota((hot_ref.shape[0], LANES), 0) == code >> 1)
    out_ref[:, SLOT_CAP:, :] = index.astype(BF16).reshape(owners, 8, LANES)

    lane_g, sub_g = iota((GROUP, LANES), 1), iota((GROUP, LANES), 0)
    for n in chunks:
        parts = []
        for j in range(0, CHUNK, GROUP):
            first = n * CHUNK + j
            if first % piece == 0:
                block_copy(first // piece).wait()
            block = blocks_ref[first : first + GROUP].reshape(GROUP * PICK_BLK, CELL_BLK)
            wide = lax.dot_general(
                rows[n][j : j + GROUP].astype(BF16), block, NT, preferred_element_type=F32
            )
            part = jnp.zeros((GROUP, LANES), F32)
            for i in range(GROUP // 2):
                own = sub_g == 2 * i + (lane_g >= PICK_BLK).astype(jnp.int32)
                part = jnp.where(own, wide[:, i * LANES : (i + 1) * LANES], part)
            parts.append(part)
        values = jnp.concatenate(parts, axis=0)
        values = values + pltpu.roll(values, PICK_BLK, 1)
        values = jnp.where((code_down[n] & 1) == half, values, 0.0)
        high, low = two_parts(values)
        values_ref[n * CHUNK : (n + 1) * CHUNK, 0:LANES] = high
        values_ref[n * CHUNK : (n + 1) * CHUNK, LANES : 2 * LANES] = low
    placed = jnp.dot(hot_ref[...], values_ref[...], preferred_element_type=F32).astype(BF16)
    q = SLOT_CAP // 2
    out_ref[:, 0:q, :] = placed[:, :LANES].reshape(owners, q, LANES)
    out_ref[:, q : 2 * q, :] = placed[:, LANES:].reshape(owners, q, LANES)


def row_matches(terms_ref):
    tile = terms_ref[:, SLOT_CAP:, :].astype(F32).reshape(-1, LANES)
    lane = (iota(tile.shape, 1) & 31).astype(F32)
    return pick(tile == lane + 1.0), pick(tile == lane + 33.0)


def stations_kernel(terms_ref, observed_ref, weight_ref, station_ref, misfit_ref, out_ref):
    rows = observed_ref.shape[0]
    q = SLOT_CAP // 2

    def part(first):
        return terms_ref[:, first : first + 8, :].astype(F32).reshape(-1, LANES).astype(BF16)

    lower, upper = [jnp.concatenate([part(t), part(q + t)], axis=1) for t in (0, 8)]
    sides = []
    for match in row_matches(terms_ref):
        low_sum = lax.dot_general(match, lower, TN, preferred_element_type=F32)
        top_sum = lax.dot_general(match, upper, TN, preferred_element_type=F32)
        low_sum = low_sum[:, :LANES] + low_sum[:, LANES:]
        top_sum = top_sum[:, :LANES] + top_sum[:, LANES:]
        sides.append((low_sum[0:32] + top_sum[32:64], low_sum[64:96] + top_sum[96:128]))
    (even_left, even_right), (odd_left, odd_right) = sides
    predicted = jnp.where(
        iota((rows, LANES), 1) < PICK_BLK,
        even_left + pltpu.roll(even_right, PICK_BLK, 1),
        odd_right + pltpu.roll(odd_left, PICK_BLK, 1),
    )
    misfit = observed_ref[...] - predicted
    misfit_ref[...] = misfit
    weight = weight_ref[...]
    stations = station_ref[...]
    high, low = stations >> 7, stations & (LANES - 1)
    hi_count = STATIONS // LANES
    pieces = [p.astype(F32) for p in three_parts(weight * misfit) + three_parts(weight)]
    total = jnp.zeros((len(pieces) * hi_count, LANES), F32)
    for r0 in range(0, rows, 8):
        left, right = [], []
        for r in range(r0, r0 + 8):
            own = iota((hi_count, LANES), 0) == high[r : r + 1]
            left.append(
                jnp.concatenate([jnp.where(own, p[r : r + 1], 0.0) for p in pieces], axis=0).astype(BF16)
            )
            right.append(pick(iota((LANES, LANES), 0) == low[r : r + 1]))
        total = total + lax.dot_general(
            jnp.concatenate(left, axis=1), jnp.concatenate(right, axis=1), NT, preferred_element_type=F32
        )
    h = hi_count
    numer = total[0:h] + total[h : 2 * h] + total[2 * h : 3 * h]
    denom = total[3 * h : 4 * h] + total[4 * h : 5 * h] + total[5 * h : 6 * h]
    for first in (0, 1):
        part = slice(first * h // 2, (first + 1) * h // 2)
        sums = jnp.concatenate([p.astype(F32) for p in two_parts(numer[part])] + [denom[part]], axis=0)
        for s in range(first, out_ref.shape[0], 2):
            out_ref[s] = sums.astype(BF16)


def spread_kernel(terms_ref, out_ref):
    total = terms_ref[0].astype(F32)
    for s in range(1, terms_ref.shape[0]):
        total = total + terms_ref[s].astype(F32)
    h = total.shape[0] // 3
    sums = jnp.concatenate([total[:h] + total[h : 2 * h], total[2 * h :]], axis=0)
    for s in range(out_ref.shape[0]):
        out_ref[s] = sums


def weighted_kernel(terms_ref, misfit_ref, weight_ref, station_ref, partials_ref, corr_ref, weighted_ref, out_ref):
    lower, upper = terms_ref[0], terms_ref[1]
    for s in range(2, terms_ref.shape[0], 2):
        lower = lower + terms_ref[s]
        upper = upper + terms_ref[s + 1]
    h = lower.shape[0] // 2
    numer = jnp.concatenate([lower[:h], upper[:h]], axis=0)
    denom = jnp.concatenate([lower[h:], upper[h:]], axis=0)
    corr = numer / (denom + 1.0)
    corr_ref[...] = corr
    stations = station_ref[...]
    high, low = stations >> 7, stations & (LANES - 1)
    found = jnp.zeros(stations.shape, F32)
    for h in range(corr.shape[0]):
        line = jnp.broadcast_to(corr[h : h + 1], stations.shape)
        found = jnp.where(high == h, jnp.take_along_axis(line, low, axis=1), found)
    weighted = weight_ref[...] * (misfit_ref[...] - found)
    weighted_ref[...] = weighted
    halves = weighted.astype(BF16).astype(F32)
    lane = iota(halves.shape, 1)
    left = lane < PICK_BLK
    turned = pltpu.roll(halves, PICK_BLK, 1)
    none = jnp.zeros_like(halves)
    tables = []
    for both in (jnp.where(left, halves, turned), jnp.where(left, turned, halves)):
        first, second = jnp.where(left, both, 0.0), jnp.where(left, 0.0, both)
        lower = jnp.concatenate([first, none, second, none], axis=0)
        upper = jnp.concatenate([none, first, none, second], axis=0)
        tables.append(jnp.concatenate([lower, upper], axis=1))
    table = jnp.concatenate(tables, axis=0).astype(BF16)
    matches = jnp.concatenate(row_matches(partials_ref), axis=1)
    sent = jnp.dot(matches, table, preferred_element_type=F32)
    peers = out_ref.shape[0]
    sent = [sent[:, t : t + LANES].reshape(peers, 8, LANES) for t in (0, LANES)]
    out_ref[...] = jnp.concatenate(sent, axis=1).astype(BF16)


def backward_kernel(code_ref, cell_ref, resid_ref, blocks_ref, corr_ref, weighted_ref,
                    keep_ref, send_ref, corr_hbm, weighted_hbm, terms_ref, sems):
    copies = [
        pltpu.make_async_copy(corr_ref, corr_hbm, sems.at[0]),
        pltpu.make_async_copy(weighted_ref, weighted_hbm, sems.at[1]),
    ]
    for copy in copies:
        copy.start()
    slots = blocks_ref.shape[0]
    lane, sub = iota((CHUNK, LANES), 1), iota((CHUNK, LANES), 0)
    sub_p = iota((2 * GROUP, LANES), 0) & (GROUP - 1)
    parity = sub & 1
    half = (lane >= PICK_BLK).astype(jnp.int32)
    for n in range(slots // CHUNK):
        code_down = down(code_ref[n : n + 1, :])
        row_of = code_down >> 1
        chosen = jnp.concatenate(
            [pick(row_of == lane + t) for t in range(0, resid_ref.shape[0], LANES)], axis=1
        )
        resid = jnp.dot(chosen, resid_ref[...], preferred_element_type=F32)
        resid = jnp.where((code_down & 1) == parity, resid, pltpu.roll(resid, PICK_BLK, 1))
        resid = jnp.where(half == parity, resid, 0.0)
        parts = []
        for j in range(0, CHUNK, 2 * GROUP):
            first = n * CHUNK + j
            both = [
                blocks_ref[k : k + GROUP].reshape(GROUP * PICK_BLK, CELL_BLK)
                for k in (first, first + GROUP)
            ]
            mine = resid[j : j + 2 * GROUP]
            wide = jnp.concatenate(
                [jnp.where((sub_p >> 1) == i, mine, 0.0) for i in range(GROUP // 2)], axis=1
            ).astype(BF16)
            terms = jnp.dot(wide, jnp.concatenate(both, axis=1), preferred_element_type=F32)
            parts += [terms[:GROUP, :LANES], terms[GROUP:, LANES:]]
        high, low = two_parts(jnp.concatenate(parts, axis=0))
        terms_ref[n * CHUNK : (n + 1) * CHUNK, 0:LANES] = high
        terms_ref[n * CHUNK : (n + 1) * CHUNK, LANES : 2 * LANES] = low
    inside = cell_ref[...]
    both = terms_ref[...]
    cells = keep_ref.shape[0]
    kept = jnp.logical_and(inside >= 0, inside < cells)
    for ref, rows in ((send_ref, jnp.where(kept, -1, inside & (cells - 1))), (keep_ref, inside)):
        hot = jnp.concatenate(
            [pick(iota((cells, LANES), 0) == rows[r : r + 1]) for r in range(slots // LANES)], axis=1
        )
        sums = jnp.dot(hot, both, preferred_element_type=F32)
        ref[...] = (sums[:, :LANES] + sums[:, LANES:]).astype(ref.dtype)
    for copy in copies:
        copy.wait()


def pair_kernel(own_ref, other_ref, out_ref):
    total = (own_ref[...] + other_ref[...].astype(F32)).astype(BF16)
    for s in range(out_ref.shape[0]):
        out_ref[s] = total


def gradient_kernel(terms_ref, out_hbm, total_ref, sems):
    pieces = sems.shape[0]
    rows = total_ref.shape[0] // pieces
    copies = []
    for n in range(pieces):
        side, start = divmod(n * rows, terms_ref.shape[1])
        total = terms_ref[side, start : start + rows, :].astype(F32)
        for s in range(side + 2, terms_ref.shape[0], 2):
            total = total + terms_ref[s, start : start + rows, :].astype(F32)
        at = pl.ds(n * rows, rows)
        total_ref[at, :] = total
        copies.append(pltpu.make_async_copy(total_ref.at[at], out_hbm.at[at], sems.at[n]))
        copies[-1].start()
    for copy in copies:
        copy.wait()


def simple(kernel, out_shape, name, **more):
    return pl.pallas_call(
        kernel,
        out_shape=out_shape,
        compiler_params=pltpu.CompilerParams(vmem_limit_bytes=VMEM_BYTES),
        name=name,
        **more,
    )


def swap(x, axis, groups=None):
    return lax.all_to_all(x, axis, 0, 0, tiled=True, axis_index_groups=groups)


def torus_groups():
    lines, planes = {}, {}
    for x, zl, y, zh, c in itertools.product(range(4), range(2), range(4), range(4), range(2)):
        flat = (x * 2 + zl) * 32 + y * 8 + zh * 2 + c
        lines.setdefault((x, y), []).append(flat)
        planes.setdefault((zl, zh), []).append(flat)
    return list(lines.values()), list(planes.values())


def forward_call(count, picks_of, cells_of, model_rows, sensitivity, shells):
    slots = sensitivity.shape[0]
    return pl.pallas_call(
        forward_kernel,
        in_specs=[OUTSIDE] * 5,
        out_specs=(INSIDE,) * 4,
        out_shape=(
            jax.ShapeDtypeStruct((shells, SLOT_CAP + 8, LANES), BF16),
            jax.ShapeDtypeStruct(sensitivity.shape, BF16),
            jax.ShapeDtypeStruct(picks_of.shape, jnp.int32),
            jax.ShapeDtypeStruct(cells_of.shape, jnp.int32),
        ),
        scratch_shapes=[
            pltpu.SMEM((1,), jnp.int32),
            pltpu.VMEM(picks_of.shape, jnp.int32),
            pltpu.VMEM(cells_of.shape, jnp.int32),
            pltpu.VMEM(model_rows.shape, BF16),
            pltpu.VMEM((slots, 2 * LANES), BF16),
            pltpu.VMEM((shells * SLOT_CAP // 2, slots), BF16),
            pltpu.SemaphoreType.DMA((4,)),
            pltpu.SemaphoreType.DMA((PIECES,)),
        ],
        compiler_params=pltpu.CompilerParams(vmem_limit_bytes=VMEM_BYTES),
        name="forward",
    )(
        count,
        *[
            pltpu.with_memory_space_constraint(v, pltpu.HBM)
            for v in (picks_of, cells_of, model_rows, sensitivity)
        ],
    )


def local(model, sensitivity, pick_block, cell_block, blk_count, observed, pick_weight, station):
    shells, events = lax.axis_size("shells"), lax.axis_size("events")
    picks_of = pick_block.reshape(-1, LANES)
    cells_of = cell_block.reshape(-1, LANES)
    model_rows = model.reshape(-1, CELL_BLK)
    observed, weight = observed.reshape(-1, LANES), pick_weight.reshape(-1, LANES)
    station = station.reshape(-1, LANES)
    own_rows = observed.shape[0]
    stat_rows = STATIONS // LANES
    shape = jax.ShapeDtypeStruct

    lines, planes = torus_groups()
    devices = ("events", "shells")

    slots = sensitivity.shape[0]
    q = SLOT_CAP // 2
    partials, blocks, codes, sides = forward_call(blk_count, picks_of, cells_of, model_rows, sensitivity, shells)
    partials = swap(partials, "shells")
    misfit, stats = simple(
        stations_kernel,
        (
            shape((own_rows, LANES), F32),
            shape((len(lines[0]), 3 * stat_rows // 2, LANES), BF16),
        ),
        "stations",
    )(partials, observed, weight, station)
    stats = swap(stats, devices, lines)
    stats = simple(spread_kernel, shape((len(planes[0]), stat_rows, LANES), F32), "spread")(stats)
    stats = swap(stats, devices, planes)
    correction, weighted, halves = simple(
        weighted_kernel,
        (
            shape((STATIONS // LANES, LANES), F32),
            shape((own_rows, LANES), F32),
            shape((shells, q, LANES), BF16),
        ),
        "weighted",
    )(stats, misfit, weight, station, partials)
    halves = swap(halves, "shells").reshape(shells * q, LANES)
    half_cells = (model_rows.shape[0] // 2, LANES)
    kept, sent, correction, weighted = simple(
        backward_kernel,
        (
            shape(half_cells, F32),
            shape(half_cells, BF16),
            shape(correction.shape, F32),
            shape(weighted.shape, F32),
        ),
        "backward",
        out_specs=(INSIDE, INSIDE, OUTSIDE, OUTSIDE),
        scratch_shapes=[pltpu.VMEM((slots, 2 * LANES), BF16), pltpu.SemaphoreType.DMA((2,))],
    )(codes, sides, halves, blocks, correction, weighted)
    other = lax.ppermute(sent, "events", [(e, e ^ 1) for e in range(events)])
    grads = simple(pair_kernel, shape((events,) + half_cells, BF16), "pair")(kept, other)
    grads = swap(grads, "events")
    gradient = simple(
        gradient_kernel,
        shape(model_rows.shape, F32),
        "gradient",
        out_specs=OUTSIDE,
        scratch_shapes=[pltpu.VMEM(model_rows.shape, F32), pltpu.SemaphoreType.DMA((4,))],
    )(grads)
    return (gradient.reshape(-1), correction.reshape(-1), weighted.reshape(-1))


def solution(mesh):
    both = P(("events", "shells"))
    placed = (P("shells"), P(("events", "shells"), None, None)) + (both,) * 6
    return jax.shard_map(
        local,
        mesh=mesh,
        in_specs=placed,
        out_specs=(P("shells"), P(), both),
        check_vma=False,
    )
```

```python
import itertools

import jax
import jax.numpy as jnp
from jax import lax
from jax.experimental import pallas as pl
from jax.experimental.pallas import tpu as pltpu
from jax.sharding import PartitionSpec as P

PICK_BLK = 64
CELL_BLK = 128
STATIONS = 2048
LANES = 128
GROUP = 8
CHUNK = 128
F32 = jnp.float32
BF16 = jnp.bfloat16
NT = (((1,), (1,)), ((), ()))
TN = (((0,), (0,)), ((), ()))
SLOT_CAP = 32
VMEM_BYTES = 40 << 20
PIECES = 4
OUTSIDE = pl.BlockSpec(memory_space=pltpu.HBM)
INSIDE = pl.BlockSpec(memory_space=pltpu.VMEM)


def iota(shape, axis):
    return lax.broadcasted_iota(jnp.int32, shape, axis)


def down(row):
    tall = jnp.broadcast_to(row.astype(F32), (LANES, LANES))
    return jnp.transpose(tall).astype(jnp.int32)


def pick(mask):
    return jnp.where(mask, 1.0, 0.0).astype(BF16)


def two_parts(x):
    high = x.astype(BF16)
    return high, (x - high.astype(F32)).astype(BF16)


def forward_kernel(count_hbm, pick_hbm, cell_hbm, model_hbm, blocks_hbm, out_ref, blocks_ref, code_ref, side_ref,
                   count, pick_ref, cell_ref, model_ref, values_ref, hot_ref, table_sems, block_sems):
    slots, cells = blocks_ref.shape[0], model_ref.shape[0]
    owners = out_ref.shape[0]
    chunks = range(slots // CHUNK)
    tables = [
        pltpu.make_async_copy(src, dst, table_sems.at[n])
        for n, (src, dst) in enumerate(
            [(count_hbm, count), (pick_hbm, pick_ref), (cell_hbm, cell_ref), (model_hbm, model_ref)]
        )
    ]
    for copy in tables:
        copy.start()
    piece = slots // block_sems.shape[0]

    def block_copy(n):
        at = pl.ds(n * piece, piece)
        return pltpu.make_async_copy(blocks_hbm.at[at], blocks_ref.at[at], block_sems.at[n])

    def start_copy(n, carry):
        block_copy(n).start()
        return carry

    lax.fori_loop(0, slots // piece, start_copy, 0)
    for copy in tables:
        copy.wait()
    lane, sub = iota((CHUNK, LANES), 1), iota((CHUNK, LANES), 0)
    half = (lane >= PICK_BLK).astype(jnp.int32)
    side_ref[...] = cell_ref[...] - (lax.axis_index("events") & 1) * (cells // 2)

    before, every = pick(sub < lane), jnp.ones((CHUNK, LANES), BF16)
    seen = jnp.zeros((owners, LANES), F32)
    index = jnp.zeros((owners * 8, LANES), F32)
    codes, code_down, rows = [], [], []
    for n in chunks:
        picks = pick_ref[n : n + 1, :]
        used = n * CHUNK + iota((1, LANES), 1) < count[0]
        owner, inside = picks >> 6, picks & (PICK_BLK - 1)
        mine = jnp.logical_and(iota((owners, LANES), 0) == owner, used)
        ones = pick(mine)
        ahead = seen + jnp.dot(ones, before, preferred_element_type=F32)
        seen = seen + jnp.dot(ones, every, preferred_element_type=F32)
        rank = jnp.sum(jnp.where(mine, ahead, 0.0), axis=0, keepdims=True).astype(jnp.int32)
        code = jnp.where(used, owner * SLOT_CAP + rank, -1)
        codes.append(code)
        code_ref[n : n + 1, :] = code
        code_down.append(down(code))
        cell_down = down(cell_ref[n : n + 1, :])
        chosen = jnp.concatenate([pick(cell_down == lane + t) for t in range(0, cells, LANES)], axis=1)
        rows.append(jnp.dot(chosen, model_ref[...], preferred_element_type=F32))
        tile_row = jnp.where(used, owner * 8 + ((code >> 1) & 7), -1)
        block = (inside & 1) * 32 + (inside >> 1) + 1
        tagged = iota((owners * 8, LANES), 0) == tile_row
        tagged = jnp.where(tagged, block.astype(F32), 0.0).astype(BF16)
        quarter = (code_down[n] & 1) * 2 + ((code_down[n] >> 4) & 1)
        index = index + jnp.dot(tagged, pick(lane >> 5 == quarter), preferred_element_type=F32)
        hot_ref[:, n * CHUNK : (n + 1) * CHUNK] = pick(iota((hot_ref.shape[0], LANES), 0) == code >> 1)
    out_ref[:, SLOT_CAP:, :] = index.astype(BF16).reshape(owners, 8, LANES)

    lane_g, sub_g = iota((GROUP, LANES), 1), iota((GROUP, LANES), 0)
    for n in chunks:
        parts = []
        for j in range(0, CHUNK, GROUP):
            first = n * CHUNK + j
            if first % piece == 0:
                block_copy(first // piece).wait()
            block = blocks_ref[first : first + GROUP].reshape(GROUP * PICK_BLK, CELL_BLK)
            wide = lax.dot_general(
                rows[n][j : j + GROUP].astype(BF16), block, NT, preferred_element_type=F32
            )
            part = jnp.zeros((GROUP, LANES), F32)
            for i in range(GROUP // 2):
                own = sub_g == 2 * i + (lane_g >= PICK_BLK).astype(jnp.int32)
                part = jnp.where(own, wide[:, i * LANES : (i + 1) * LANES], part)
            parts.append(part)
        values = jnp.concatenate(parts, axis=0)
        values = values + pltpu.roll(values, PICK_BLK, 1)
        values = jnp.where((code_down[n] & 1) == half, values, 0.0)
        high, low = two_parts(values)
        values_ref[n * CHUNK : (n + 1) * CHUNK, 0:LANES] = high
        values_ref[n * CHUNK : (n + 1) * CHUNK, LANES : 2 * LANES] = low
    placed = jnp.dot(hot_ref[...], values_ref[...], preferred_element_type=F32).astype(BF16)
    q = SLOT_CAP // 2
    out_ref[:, 0:q, :] = placed[:, :LANES].reshape(owners, q, LANES)
    out_ref[:, q : 2 * q, :] = placed[:, LANES:].reshape(owners, q, LANES)


def row_matches(terms_ref):
    tile = terms_ref[:, SLOT_CAP:, :].astype(F32).reshape(-1, LANES)
    lane = (iota(tile.shape, 1) & 31).astype(F32)
    return pick(tile == lane + 1.0), pick(tile == lane + 33.0)


def stations_kernel(terms_ref, observed_ref, weight_ref, station_ref, misfit_ref, out_ref):
    rows = observed_ref.shape[0]
    q = SLOT_CAP // 2

    def part(first):
        return terms_ref[:, first : first + 8, :].astype(F32).reshape(-1, LANES).astype(BF16)

    lower, upper = [jnp.concatenate([part(t), part(q + t)], axis=1) for t in (0, 8)]
    sides = []
    for match in row_matches(terms_ref):
        low_sum = lax.dot_general(match, lower, TN, preferred_element_type=F32)
        top_sum = lax.dot_general(match, upper, TN, preferred_element_type=F32)
        low_sum = low_sum[:, :LANES] + low_sum[:, LANES:]
        top_sum = top_sum[:, :LANES] + top_sum[:, LANES:]
        sides.append((low_sum[0:32] + top_sum[32:64], low_sum[64:96] + top_sum[96:128]))
    (even_left, even_right), (odd_left, odd_right) = sides
    predicted = jnp.where(
        iota((rows, LANES), 1) < PICK_BLK,
        even_left + pltpu.roll(even_right, PICK_BLK, 1),
        odd_right + pltpu.roll(odd_left, PICK_BLK, 1),
    )
    misfit = observed_ref[...] - predicted
    misfit_ref[...] = misfit
    weight = weight_ref[...]
    stations = station_ref[...]
    high, low = stations >> 7, stations & (LANES - 1)
    hi_count = STATIONS // LANES
    pieces = [p.astype(F32) for p in two_parts(weight * misfit) + two_parts(weight)]
    total = jnp.zeros((len(pieces) * hi_count, LANES), F32)
    for r0 in range(0, rows, 8):
        left, right = [], []
        for r in range(r0, r0 + 8):
            own = iota((hi_count, LANES), 0) == high[r : r + 1]
            left.append(
                jnp.concatenate([jnp.where(own, p[r : r + 1], 0.0) for p in pieces], axis=0).astype(BF16)
            )
            right.append(pick(iota((LANES, LANES), 0) == low[r : r + 1]))
        total = total + lax.dot_general(
            jnp.concatenate(left, axis=1), jnp.concatenate(right, axis=1), NT, preferred_element_type=F32
        )
    h = hi_count
    numer = total[0:h] + total[h : 2 * h]
    denom = total[2 * h : 3 * h] + total[3 * h : 4 * h]
    for first in (0, 1):
        part = slice(first * h // 2, (first + 1) * h // 2)
        sums = jnp.concatenate([p.astype(F32) for p in two_parts(numer[part])] + [denom[part]], axis=0)
        for s in range(first, out_ref.shape[0], 2):
            out_ref[s] = sums.astype(BF16)


def spread_kernel(terms_ref, out_ref):
    total = terms_ref[0].astype(F32)
    for s in range(1, terms_ref.shape[0]):
        total = total + terms_ref[s].astype(F32)
    h = total.shape[0] // 3
    sums = jnp.concatenate([total[:h] + total[h : 2 * h], total[2 * h :]], axis=0)
    for s in range(out_ref.shape[0]):
        out_ref[s] = sums


def weighted_kernel(terms_ref, misfit_ref, weight_ref, station_ref, partials_ref, corr_ref, weighted_ref, out_ref):
    lower, upper = terms_ref[0], terms_ref[1]
    for s in range(2, terms_ref.shape[0], 2):
        lower = lower + terms_ref[s]
        upper = upper + terms_ref[s + 1]
    h = lower.shape[0] // 2
    numer = jnp.concatenate([lower[:h], upper[:h]], axis=0)
    denom = jnp.concatenate([lower[h:], upper[h:]], axis=0)
    corr = numer / (denom + 1.0)
    corr_ref[...] = corr
    stations = station_ref[...]
    high, low = stations >> 7, stations & (LANES - 1)
    found = jnp.zeros(stations.shape, F32)
    for h in range(corr.shape[0]):
        line = jnp.broadcast_to(corr[h : h + 1], stations.shape)
        found = jnp.where(high == h, jnp.take_along_axis(line, low, axis=1), found)
    weighted = weight_ref[...] * (misfit_ref[...] - found)
    weighted_ref[...] = weighted
    halves = weighted.astype(BF16).astype(F32)
    lane = iota(halves.shape, 1)
    left = lane < PICK_BLK
    turned = pltpu.roll(halves, PICK_BLK, 1)
    none = jnp.zeros_like(halves)
    tables = []
    for both in (jnp.where(left, halves, turned), jnp.where(left, turned, halves)):
        first, second = jnp.where(left, both, 0.0), jnp.where(left, 0.0, both)
        lower = jnp.concatenate([first, none, second, none], axis=0)
        upper = jnp.concatenate([none, first, none, second], axis=0)
        tables.append(jnp.concatenate([lower, upper], axis=1))
    table = jnp.concatenate(tables, axis=0).astype(BF16)
    matches = jnp.concatenate(row_matches(partials_ref), axis=1)
    sent = jnp.dot(matches, table, preferred_element_type=F32)
    peers = out_ref.shape[0]
    sent = [sent[:, t : t + LANES].reshape(peers, 8, LANES) for t in (0, LANES)]
    out_ref[...] = jnp.concatenate(sent, axis=1).astype(BF16)


def backward_kernel(code_ref, cell_ref, resid_ref, blocks_ref, corr_ref, weighted_ref,
                    keep_ref, send_ref, corr_hbm, weighted_hbm, terms_ref, sems):
    copies = [
        pltpu.make_async_copy(corr_ref, corr_hbm, sems.at[0]),
        pltpu.make_async_copy(weighted_ref, weighted_hbm, sems.at[1]),
    ]
    for copy in copies:
        copy.start()
    slots = blocks_ref.shape[0]
    lane, sub = iota((CHUNK, LANES), 1), iota((CHUNK, LANES), 0)
    sub_p = iota((2 * GROUP, LANES), 0) & (GROUP - 1)
    parity = sub & 1
    half = (lane >= PICK_BLK).astype(jnp.int32)
    for n in range(slots // CHUNK):
        code_down = down(code_ref[n : n + 1, :])
        row_of = code_down >> 1
        chosen = jnp.concatenate(
            [pick(row_of == lane + t) for t in range(0, resid_ref.shape[0], LANES)], axis=1
        )
        resid = jnp.dot(chosen, resid_ref[...], preferred_element_type=F32)
        resid = jnp.where((code_down & 1) == parity, resid, pltpu.roll(resid, PICK_BLK, 1))
        resid = jnp.where(half == parity, resid, 0.0)
        parts = []
        for j in range(0, CHUNK, 2 * GROUP):
            first = n * CHUNK + j
            both = [
                blocks_ref[k : k + GROUP].reshape(GROUP * PICK_BLK, CELL_BLK)
                for k in (first, first + GROUP)
            ]
            mine = resid[j : j + 2 * GROUP]
            wide = jnp.concatenate(
                [jnp.where((sub_p >> 1) == i, mine, 0.0) for i in range(GROUP // 2)], axis=1
            ).astype(BF16)
            terms = jnp.dot(wide, jnp.concatenate(both, axis=1), preferred_element_type=F32)
            parts += [terms[:GROUP, :LANES], terms[GROUP:, LANES:]]
        high, low = two_parts(jnp.concatenate(parts, axis=0))
        terms_ref[n * CHUNK : (n + 1) * CHUNK, 0:LANES] = high
        terms_ref[n * CHUNK : (n + 1) * CHUNK, LANES : 2 * LANES] = low
    inside = cell_ref[...]
    both = terms_ref[...]
    cells = keep_ref.shape[0]
    kept = jnp.logical_and(inside >= 0, inside < cells)
    for ref, rows in ((send_ref, jnp.where(kept, -1, inside & (cells - 1))), (keep_ref, inside)):
        hot = jnp.concatenate(
            [pick(iota((cells, LANES), 0) == rows[r : r + 1]) for r in range(slots // LANES)], axis=1
        )
        sums = jnp.dot(hot, both, preferred_element_type=F32)
        ref[...] = (sums[:, :LANES] + sums[:, LANES:]).astype(ref.dtype)
    for copy in copies:
        copy.wait()


def pair_kernel(own_ref, other_ref, out_ref):
    total = (own_ref[...] + other_ref[...].astype(F32)).astype(BF16)
    for s in range(out_ref.shape[0]):
        out_ref[s] = total


def gradient_kernel(terms_ref, out_hbm, total_ref, sems):
    pieces = sems.shape[0]
    rows = total_ref.shape[0] // pieces
    copies = []
    for n in range(pieces):
        side, start = divmod(n * rows, terms_ref.shape[1])
        total = terms_ref[side, start : start + rows, :].astype(F32)
        for s in range(side + 2, terms_ref.shape[0], 2):
            total = total + terms_ref[s, start : start + rows, :].astype(F32)
        at = pl.ds(n * rows, rows)
        total_ref[at, :] = total
        copies.append(pltpu.make_async_copy(total_ref.at[at], out_hbm.at[at], sems.at[n]))
        copies[-1].start()
    for copy in copies:
        copy.wait()


def simple(kernel, out_shape, name, **more):
    return pl.pallas_call(
        kernel,
        out_shape=out_shape,
        compiler_params=pltpu.CompilerParams(vmem_limit_bytes=VMEM_BYTES),
        name=name,
        **more,
    )


def swap(x, axis, groups=None):
    return lax.all_to_all(x, axis, 0, 0, tiled=True, axis_index_groups=groups)


def torus_groups():
    lines, planes = {}, {}
    for x, zl, y, zh, c in itertools.product(range(4), range(2), range(4), range(4), range(2)):
        flat = (x * 2 + zl) * 32 + y * 8 + zh * 2 + c
        lines.setdefault((x, y), []).append(flat)
        planes.setdefault((zl, zh), []).append(flat)
    return list(lines.values()), list(planes.values())


def forward_call(count, picks_of, cells_of, model_rows, sensitivity, shells):
    slots = sensitivity.shape[0]
    return pl.pallas_call(
        forward_kernel,
        in_specs=[OUTSIDE] * 5,
        out_specs=(INSIDE,) * 4,
        out_shape=(
            jax.ShapeDtypeStruct((shells, SLOT_CAP + 8, LANES), BF16),
            jax.ShapeDtypeStruct(sensitivity.shape, BF16),
            jax.ShapeDtypeStruct(picks_of.shape, jnp.int32),
            jax.ShapeDtypeStruct(cells_of.shape, jnp.int32),
        ),
        scratch_shapes=[
            pltpu.SMEM((1,), jnp.int32),
            pltpu.VMEM(picks_of.shape, jnp.int32),
            pltpu.VMEM(cells_of.shape, jnp.int32),
            pltpu.VMEM(model_rows.shape, BF16),
            pltpu.VMEM((slots, 2 * LANES), BF16),
            pltpu.VMEM((shells * SLOT_CAP // 2, slots), BF16),
            pltpu.SemaphoreType.DMA((4,)),
            pltpu.SemaphoreType.DMA((PIECES,)),
        ],
        compiler_params=pltpu.CompilerParams(vmem_limit_bytes=VMEM_BYTES),
        name="forward",
    )(
        count,
        *[
            pltpu.with_memory_space_constraint(v, pltpu.HBM)
            for v in (picks_of, cells_of, model_rows, sensitivity)
        ],
    )


def local(model, sensitivity, pick_block, cell_block, blk_count, observed, pick_weight, station):
    shells, events = lax.axis_size("shells"), lax.axis_size("events")
    picks_of = pick_block.reshape(-1, LANES)
    cells_of = cell_block.reshape(-1, LANES)
    model_rows = model.reshape(-1, CELL_BLK)
    observed, weight = observed.reshape(-1, LANES), pick_weight.reshape(-1, LANES)
    station = station.reshape(-1, LANES)
    own_rows = observed.shape[0]
    stat_rows = STATIONS // LANES
    shape = jax.ShapeDtypeStruct

    lines, planes = torus_groups()
    devices = ("events", "shells")

    slots = sensitivity.shape[0]
    q = SLOT_CAP // 2
    partials, blocks, codes, sides = forward_call(blk_count, picks_of, cells_of, model_rows, sensitivity, shells)
    partials = swap(partials, "shells")
    misfit, stats = simple(
        stations_kernel,
        (
            shape((own_rows, LANES), F32),
            shape((len(lines[0]), 3 * stat_rows // 2, LANES), BF16),
        ),
        "stations",
    )(partials, observed, weight, station)
    stats = swap(stats, devices, lines)
    stats = simple(spread_kernel, shape((len(planes[0]), stat_rows, LANES), F32), "spread")(stats)
    stats = swap(stats, devices, planes)
    correction, weighted, halves = simple(
        weighted_kernel,
        (
            shape((STATIONS // LANES, LANES), F32),
            shape((own_rows, LANES), F32),
            shape((shells, q, LANES), BF16),
        ),
        "weighted",
    )(stats, misfit, weight, station, partials)
    halves = swap(halves, "shells").reshape(shells * q, LANES)
    half_cells = (model_rows.shape[0] // 2, LANES)
    kept, sent, correction, weighted = simple(
        backward_kernel,
        (
            shape(half_cells, F32),
            shape(half_cells, BF16),
            shape(correction.shape, F32),
            shape(weighted.shape, F32),
        ),
        "backward",
        out_specs=(INSIDE, INSIDE, OUTSIDE, OUTSIDE),
        scratch_shapes=[pltpu.VMEM((slots, 2 * LANES), BF16), pltpu.SemaphoreType.DMA((2,))],
    )(codes, sides, halves, blocks, correction, weighted)
    other = lax.ppermute(sent, "events", [(e, e ^ 1) for e in range(events)])
    grads = simple(pair_kernel, shape((events,) + half_cells, BF16), "pair")(kept, other)
    grads = swap(grads, "events")
    gradient = simple(
        gradient_kernel,
        shape(model_rows.shape, F32),
        "gradient",
        out_specs=OUTSIDE,
        scratch_shapes=[pltpu.VMEM(model_rows.shape, F32), pltpu.SemaphoreType.DMA((4,))],
    )(grads)
    return (gradient.reshape(-1), correction.reshape(-1), weighted.reshape(-1))


def solution(mesh):
    both = P(("events", "shells"))
    placed = (P("shells"), P(("events", "shells"), None, None)) + (both,) * 6
    return jax.shard_map(
        local,
        mesh=mesh,
        in_specs=placed,
        out_specs=(P("shells"), P(), both),
        check_vma=False,
    )
```
